256 devices in a mesh: vert: 128 (over y_hi, x, z, core), sa: 2 (over y_lo).
Axes of the slice: x: 4, y: 4 (y_hi: 2, y_lo: 2; y = y_hi * 2 + y_lo), z: 8, core: 2. Of those that a mesh axis runs over, the one named last changes fastest.
Arguments:
- state: bfloat16 [2048, 32, 1024], P('vert', 'sa'), may hold values from -6 to 6
- cotangent: bfloat16 [2048, 32, 1024], P('vert', 'sa'), may hold values from -6 to 6
- collision: bfloat16 [2048, 2048], replicated, may hold values from -0.125 to 0.125
- wall_shape: float32 [2048], replicated, may hold values from 0.5 to 2
- flux_weight: float32 [2048], replicated, may hold values from -0.125 to 0.125
- courant: float32 [3, 2048], P(None, 'vert'), may hold values from 0.03 to 0.3
- upwind_bits: int32 [3, 2048], P(None, 'vert'), may hold values from 0 to 1
- accommodation: float32 [256, 128], P(('vert', 'sa')), may hold values from 0.2 to 1
- wall_flags: int32 [256, 128], P(('vert', 'sa')), may hold values 0 or 1
Outputs:
- advanced: bfloat16 [2048, 32, 1024], P('vert', 'sa')
- previous: bfloat16 [2048, 32, 1024], P('vert', 'sa')
- sensitivity: float32 [256, 128], P(('vert', 'sa'))
The draws below stay inside these ranges and needn't reach their ends.
All inputs are finite; a program needn't handle non-finite values. No bound on the sum of `wall_flags` on one device may be relied on, other than what follows from the above.
Results may differ from the reference program's by a relative error of at most 0.0051.
Values may be sent and summed in bfloat16 or wider, within the bound.
A program may use at most 64 MiB of HBM per device.

```python
import math
import jax
import jax.numpy as jnp
from jax import lax

V = 2048
NY = 32
NZ = 32
NX = 32
CB = 128
N_VERT = 128
N_SA = 2


def set_ends(values, rng, low, largest):
    longest = values.shape.index(max(values.shape))
    spots = []
    for shift in (0, 1):
        where = [jax.random.randint(jax.random.fold_in(rng, axis), (), 0, length) for axis, length in enumerate(values.shape)]
        where[longest] = (where[longest] + shift) % values.shape[longest]
        spots.append(tuple(where))
    return values.at[spots[0]].set(low).at[spots[1]].set(largest)


def block_scale(stream_key, dims, shards, low, largest):
    level, own = 1.0, jax.random.fold_in(stream_key, 6)
    for position, shards_of in shards:
        steps = jnp.exp(jax.random.uniform(jax.random.fold_in(own, position), (shards_of,), jnp.float32, low / len(shards), largest / len(shards)))
        level = level * jnp.repeat(steps, dims[position] // shards_of).reshape([-1 if axis == position else 1 for axis in range(len(dims))])
    return level


def bell_draw(own_key, extent, width, bound, cuts=(), kind=jnp.bfloat16):
    values = width * jax.random.normal(own_key, extent, jnp.float32)
    if cuts:
        values = values * block_scale(own_key, extent, cuts, -0.22, 0.18)
    return jnp.clip(values, -bound, bound).astype(kind)


def setup_inputs(seed: int = 0) -> dict:
    splits = jax.random.split(jax.random.key(seed), 10)
    return {
        "state": bell_draw(splits[0], (V, NX, NY * NZ), 1.0, 6.0, ((0, 128), (1, 2))),
        "cotangent": bell_draw(splits[1], (V, NX, NY * NZ), 1.0, 6.0, ((0, 128), (1, 2))),
        "collision": bell_draw(splits[2], (V, V), V ** -0.5, 0.125),
        "wall_shape": jnp.clip(jnp.exp(jax.random.uniform(splits[3], (V,), jnp.float32, math.log(0.5), math.log(2.0))), 0.5, 2.0),
        "flux_weight": bell_draw(splits[4], (V,), V ** -0.5, 0.125, (), jnp.float32),
        "courant": jnp.clip(jnp.exp(math.log(0.3) - 2.3025852 * jax.random.uniform(splits[5], (3, V), jnp.float32) ** block_scale(splits[5], (3, V), ((1, 128),), -0.2, 0.2)), 0.03, 0.3),
        "upwind_bits": set_ends(jax.random.randint(splits[6], (3, V), 0, 2), jax.random.fold_in(splits[6], 1), 0, 1).astype(jnp.int32),
        "accommodation": jnp.clip(0.2 + 0.8 * jax.random.uniform(splits[7], (N_VERT * N_SA, CB), jnp.float32) ** block_scale(splits[7], (N_VERT * N_SA, CB), ((0, 256),), -0.2, 0.2), 0.2, 1.0),
        "wall_flags": set_ends((jax.random.randint(splits[8], (N_VERT * N_SA, CB), 0, 4) < 1).astype(jnp.int32), jax.random.fold_in(splits[8], 1), 0, 1),
    }


def neighbour_pairs(padded, z_cells):
    middle = padded[:, 1:-1]
    plane_len = middle.shape[2]
    z_index = lax.broadcasted_iota(jnp.int32, (1, 1, plane_len), 2) % z_cells
    wide_y = jnp.pad(middle, ((0, 0), (0, 0), (z_cells, z_cells)))
    wide_z = jnp.pad(middle, ((0, 0), (0, 0), (1, 1)))
    zero_val = jnp.zeros((), middle.dtype)
    minus_side = (padded[:, :-2], wide_y[:, :, :plane_len],
                  jnp.where(z_index != 0, wide_z[:, :, :plane_len], zero_val))
    plus_side = (padded[:, 2:], wide_y[:, :, 2 * z_cells:],
                 jnp.where(z_index != z_cells - 1, wide_z[:, :, 2:], zero_val))
    return middle, minus_side, plus_side


def transport(padded, courant, upwind, z_cells, forward):
    middle, minus_side, plus_side = neighbour_pairs(padded, z_cells)
    central = middle.astype(jnp.float32)
    result = central
    for axis_num in range(3):
        speed_ratio = courant[axis_num][:, None, None]
        upward = upwind[axis_num][:, None, None] == 1
        if forward:
            donor = jnp.where(upward, minus_side[axis_num], plus_side[axis_num])
        else:
            donor = jnp.where(upward, plus_side[axis_num], minus_side[axis_num])
        result = result - speed_ratio * (central - donor.astype(jnp.float32))
    return result


def collide_forward(passed, collision, wall_shape, flux_weight, gain):
    moved = passed.astype(jnp.float32)
    density = jnp.sum(flux_weight[:, None] * moved, axis=0, keepdims=True)
    target = wall_shape[:, None] * density - moved
    relaxed = moved + gain * target
    relaxed_half = relaxed.astype(jnp.bfloat16)
    mixed = lax.dot_general(collision, relaxed_half, (((0,), (0,)), ((), ())),
                            preferred_element_type=jnp.float32)
    advanced = (relaxed + mixed).astype(jnp.bfloat16)
    return advanced, target


def collide_adjoint(adjoint_in, collision, wall_shape, flux_weight, gain, flags_row, target):
    adjoint_h = adjoint_in.astype(jnp.float32) + jnp.dot(collision, adjoint_in,
                                                         preferred_element_type=jnp.float32)
    weighted = jnp.sum(wall_shape[:, None] * adjoint_h, axis=0, keepdims=True)
    adjoint_g = (adjoint_h + gain * (flux_weight[:, None] * weighted - adjoint_h)).astype(jnp.bfloat16)
    sensitivity = flags_row * jnp.sum(adjoint_h * target, axis=0, keepdims=True)
    return adjoint_g, sensitivity


def blocks_to_grid(blocked):
    spread = jnp.transpose(blocked.reshape(N_VERT, N_SA, CB), (1, 0, 2))
    return spread.reshape(NX, NY * NZ)


def grid_to_blocks(grid):
    spread = jnp.transpose(grid.reshape(N_SA, N_VERT, CB), (1, 0, 2))
    return spread.reshape(N_VERT * N_SA, CB)


def reference(state, cotangent, collision, wall_shape, flux_weight, courant, upwind_bits, accommodation, wall_flags):
    rim = ((0, 0), (1, 1), (0, 0))
    passed = transport(jnp.pad(state, rim), courant, upwind_bits, NZ, True).astype(jnp.bfloat16)
    flags_all = blocks_to_grid(wall_flags.astype(jnp.float32))
    acc_grid = blocks_to_grid(accommodation)

    def per_plane(items):
        plane_state, plane_cot, plane_acc, plane_flags = items
        gain = plane_acc[None, :] * plane_flags[None, :]
        advanced, target = collide_forward(plane_state, collision, wall_shape, flux_weight, gain)
        adjoint_g, sensitivity = collide_adjoint(plane_cot, collision, wall_shape, flux_weight,
                                                 gain, plane_flags[None, :], target)
        return advanced, adjoint_g, sensitivity[0]

    advanced, adjoint_g, sensitivity = lax.map(
        per_plane, (jnp.moveaxis(passed, 1, 0), jnp.moveaxis(cotangent, 1, 0), acc_grid, flags_all))
    advanced = jnp.moveaxis(advanced, 0, 1)
    adjoint_g = jnp.moveaxis(adjoint_g, 0, 1)
    previous = transport(jnp.pad(adjoint_g, rim), courant, upwind_bits, NZ, False).astype(jnp.bfloat16)
    return advanced, previous, grid_to_blocks(sensitivity)
```

```python
import jax
import jax.numpy as jnp
from jax import lax
from jax.experimental import pallas as pl
from jax.experimental.pallas import tpu as pltpu
from jax.sharding import PartitionSpec as P

MESH = pl.DeviceIdType.MESH
F32 = jnp.float32
BF16 = jnp.bfloat16
NZ = 32
LANES = 128
VL = 16
SLAB = 16
YB = 8
NB = SLAB * YB
TILE = 256
PER = TILE // VL
NT = 2048 // TILE


def column(row, n):
    r = lax.broadcasted_iota(jnp.int32, (n, n), 0)
    c = lax.broadcasted_iota(jnp.int32, (n, n), 1)
    one = jnp.sum(jnp.where(r == c, jnp.broadcast_to(row, (n, n)), 0.0), axis=1, keepdims=True)
    return jnp.broadcast_to(one, (n, LANES))


def step_kernel(
    state_ref, cot_ref, coll_ref, shape_ref, flux_ref, cour_ref, bits_ref, acc_ref, flag_ref,
    adv_ref, prev_ref, sens_ref,
    svm, cvm, cmat, turn, halo_s, halo_g,
    cot_s, pas_s, adj_s, adv_s, cot_r, pas_r, adv_r,
    ws, wf, hbuf, xbuf, rt, coef, masks,
    load_sem, send_sem, recv_sem, face_ss, face_rs,
):
    me = lax.axis_index("vert")
    sa = lax.axis_index("sa")
    my_tile, my_pos = me // PER, me % PER

    loads = [
        pltpu.make_async_copy(cot_ref, cvm, load_sem.at[0]),
        pltpu.make_async_copy(state_ref, svm, load_sem.at[1]),
        pltpu.make_async_copy(coll_ref, cmat, load_sem.at[2]),
    ]
    for c in loads:
        c.start()

    def peer(tile, pos):
        return ((my_tile + tile) % NT) * PER + (my_pos + pos) % PER

    barrier = pltpu.get_barrier_semaphore()
    pl.semaphore_signal(barrier, inc=1, device_id={"sa": 1 - sa}, device_id_type=MESH)

    def greet(k, _):
        pl.semaphore_signal(
            barrier, inc=1, device_id={"vert": peer(k // PER, k % PER)}, device_id_type=MESH
        )
        return 0

    lax.fori_loop(1, NB, greet, 0)

    for d in range(3):
        coef[d] = column(cour_ref[d : d + 1, :], VL)
        masks[d] = column(bits_ref[d : d + 1, :].astype(F32), VL)
    zero_plane = jnp.zeros((YB, VL, LANES), BF16)
    lone = sa * (NB + YB)
    halo_s[pl.ds(lone, YB)] = zero_plane
    halo_g[pl.ds(lone, YB)] = zero_plane

    def to_blocks(src, dst, base):
        def rows_in(v, _):
            plane = src[v].astype(F32)
            for j in range(YB):
                turn[j, pl.ds(v, SLAB, stride=VL), :] = plane[:, j * LANES : (j + 1) * LANES]
            return 0

        lax.fori_loop(0, VL, rows_in, 0, unroll=4)

        def planes_out(x, _):
            for j in range(YB):
                part = turn[j, pl.ds(pl.multiple_of(x * VL, VL), VL), :]
                dst[base + x * YB + j] = part.astype(BF16)
            return 0

        lax.fori_loop(0, SLAB, planes_out, 0, unroll=2)

    def send(src, src_base, dst, dst_base, phase, tile, pos):
        d = peer(tile, pos)
        pltpu.make_async_remote_copy(
            src_ref=src.at[src_base + d],
            dst_ref=dst.at[dst_base + me],
            send_sem=send_sem.at[phase],
            recv_sem=recv_sem.at[phase],
            device_id={"vert": d},
            device_id_type=MESH,
        ).start()

    def send_tile(src, src_base, dst, dst_base, phase, tile):
        def one(pos, _):
            send(src, src_base, dst, dst_base, phase, tile, pos)
            return 0

        lax.fori_loop(1 - jnp.minimum(tile, 1), PER, one, 0)

    def send_all(src, src_base, dst, dst_base, phase):
        def one(k, _):
            send(src, src_base, dst, dst_base, phase, k // PER, k % PER)
            return 0

        lax.fori_loop(1, NB, one, 0)

    def wait_blocks(ref, sem):
        part = ref.at[pl.ds(0, NB - 1)]
        pltpu.make_async_copy(part, part, sem).wait()

    def face(buf, k):
        return pltpu.make_async_remote_copy(
            src_ref=buf.at[pl.ds(YB + (NB - YB) * (1 - sa), YB)],
            dst_ref=buf.at[pl.ds((NB + YB) * sa, YB)],
            send_sem=face_ss.at[k],
            recv_sem=face_rs.at[k],
            device_id={"sa": 1 - sa},
            device_id_type=MESH,
        )

    lane = lax.broadcasted_iota(jnp.int32, (VL, LANES), 1)
    z_at = lane % NZ

    def transport(buf, forward, emit):
        def plane(x, _):
            base = x * YB
            mid = [buf[base + YB + j].astype(F32) for j in range(YB)]
            up32 = [pltpu.roll(m, NZ, 1) for m in mid]
            dn32 = [pltpu.roll(m, LANES - NZ, 1) for m in mid]
            zero = jnp.zeros((VL, LANES), F32)
            for j in range(YB):
                m = mid[j]
                minus = (
                    buf[base + j].astype(F32),
                    jnp.where(lane < NZ, up32[j - 1] if j else zero, up32[j]),
                    jnp.where(z_at != 0, pltpu.roll(m, 1, 1), 0.0),
                )
                plus = (
                    buf[base + 2 * YB + j].astype(F32),
                    jnp.where(lane >= LANES - NZ, dn32[j + 1] if j < YB - 1 else zero, dn32[j]),
                    jnp.where(z_at != NZ - 1, pltpu.roll(m, LANES - 1, 1), 0.0),
                )
                res = m
                for d in range(3):
                    up = masks[d] == 1.0
                    donor = jnp.where(up, minus[d], plus[d]) if forward else jnp.where(up, plus[d], minus[d])
                    res = res - coef[d] * (m - donor)
                emit(x, j, res)
            return 0

        lax.fori_loop(0, SLAB, plane, 0)

    def out_rows(dst):
        def one(v, _):
            for j in range(YB):
                rows = turn[j, pl.ds(pl.multiple_of(v * SLAB, SLAB), SLAB), :]
                dst[v, :, j * LANES : (j + 1) * LANES] = rows.astype(BF16)
            return 0

        lax.fori_loop(0, VL, one, 0, unroll=2)

    loads[0].wait()
    to_blocks(cvm, cot_s, 0)
    loads[1].wait()
    to_blocks(svm, halo_s, YB)

    pl.semaphore_wait(barrier, NB)
    face_s = face(halo_s, 0)
    face_s.start()
    send_all(cot_s, 0, cot_r, 0, 0)
    cot_r[me] = cot_s[me]

    face_s.wait()

    def emit_passed(x, j, res):
        pas_s[x * YB + j] = res.astype(BF16)

    transport(halo_s, True, emit_passed)
    send_all(pas_s, 0, pas_r, 0, 1)
    pas_r[me] = pas_s[me]

    def spread(g, _):
        rows = pl.ds(pl.multiple_of(g * LANES, LANES), LANES)
        ws[rows, :] = jnp.broadcast_to(shape_ref[pl.ds(g, 1), :], (LANES, LANES)).T
        wf[rows, :] = jnp.broadcast_to(flux_ref[pl.ds(g, 1), :], (LANES, LANES)).T
        return 0

    lax.fori_loop(0, 2048 // LANES, spread, 0)
    flags = flag_ref[...].astype(F32)
    gain = acc_ref[...] * flags

    def tile_rows(t):
        return pl.ds(pl.multiple_of(t * TILE, TILE), TILE)

    def tile_blocks(t):
        return pl.ds(pl.multiple_of(t * PER, PER), PER)

    def fold(a):
        return jnp.sum(a.reshape(TILE // 8, 8, LANES), axis=0)

    loads[2].wait()
    wait_blocks(cot_r, recv_sem.at[0])
    cot_all = cot_r.reshape(2048, LANES)

    def adjoint_tile(t, total):
        rows = tile_rows(t)
        h = jnp.dot(cmat[rows, :], cot_all[...], preferred_element_type=F32)
        h = cot_all[rows, :].astype(F32) + h
        hbuf[rows, :] = h
        return total + fold(ws[rows, :] * h)

    total = lax.fori_loop(0, NT, adjoint_tile, jnp.zeros((8, LANES), F32))
    weighted = jnp.sum(total, axis=0, keepdims=True)

    def adjoint_out(k, _):
        t = (my_tile + k) % NT
        rows = tile_rows(t)
        h = hbuf[rows, :]
        g = h + gain * (wf[rows, :] * weighted - h)
        adj_s[tile_blocks(t)] = g.astype(BF16).reshape(PER, VL, LANES)
        return 0

    lax.fori_loop(0, NT, adjoint_out, 0)
    send_all(adj_s, 0, halo_g, YB, 2)
    halo_g[YB + me] = adj_s[me]

    wait_blocks(pas_r, recv_sem.at[1])
    pas_all = pas_r.reshape(2048, LANES)

    def density_tile(t, total):
        rows = tile_rows(t)
        return total + fold(wf[rows, :] * pas_all[rows, :].astype(F32))

    total = lax.fori_loop(0, NT, density_tile, jnp.zeros((8, LANES), F32))
    density = jnp.sum(total, axis=0, keepdims=True)

    def relax_block(g, total):
        rows = pl.ds(pl.multiple_of(g * LANES, LANES), LANES)
        moved = pas_all[rows, :].astype(F32)
        target = ws[rows, :] * density - moved
        relaxed = moved + gain * target
        xbuf[rows, :] = relaxed
        rt[:, rows] = relaxed.T.astype(BF16)
        return total + jnp.sum((hbuf[rows, :] * target).reshape(LANES // 8, 8, LANES), axis=0)

    total = lax.fori_loop(0, 2048 // LANES, relax_block, jnp.zeros((8, LANES), F32))
    sens_ref[...] = flags * jnp.sum(total, axis=0, keepdims=True)

    def forward_tile(k, _):
        t = (my_tile + k) % NT
        rows = tile_rows(t)
        mixed = jnp.dot(rt[...], cmat[:, rows], preferred_element_type=F32)
        adv = xbuf[rows, :] + mixed.T
        adv_s[tile_blocks(t)] = adv.astype(BF16).reshape(PER, VL, LANES)

        @pl.when(k > 0)
        def _():
            send_tile(adv_s, 0, adv_r, 0, 3, k - 1)

        return 0

    lax.fori_loop(0, NT, forward_tile, 0)
    send_tile(adv_s, 0, adv_r, 0, 3, NT - 1)
    adv_r[me] = adv_s[me]

    wait_blocks(halo_g, recv_sem.at[2])
    face_g = face(halo_g, 1)
    face_g.start()
    face_g.wait()

    def emit_previous(x, j, res):
        turn[j, pl.ds(x, VL, stride=SLAB), :] = res

    transport(halo_g, False, emit_previous)
    out_rows(prev_ref)

    wait_blocks(adv_r, recv_sem.at[3])

    def unpack(x, _):
        for j in range(YB):
            turn[j, pl.ds(x, VL, stride=SLAB), :] = adv_r[x * YB + j].astype(F32)
        return 0

    lax.fori_loop(0, SLAB, unpack, 0, unroll=2)
    out_rows(adv_ref)

    for phase, buf in enumerate((cot_s, pas_s, adj_s, adv_s)):
        wait_blocks(buf, send_sem.at[phase])


def body(state, cotangent, collision, wall_shape, flux_weight, courant, upwind_bits, accommodation, wall_flags):
    vm = pl.BlockSpec(memory_space=pltpu.VMEM)
    hb = pl.BlockSpec(memory_space=pl.ANY)
    blocks = pltpu.VMEM((NB, VL, LANES), BF16)
    full = pltpu.VMEM((2048, LANES), F32)
    return pl.pallas_call(
        step_kernel,
        name="step",
        out_shape=(
            jax.ShapeDtypeStruct(state.shape, BF16),
            jax.ShapeDtypeStruct(state.shape, BF16),
            jax.ShapeDtypeStruct(accommodation.shape, F32),
        ),
        in_specs=[hb, hb, hb] + [vm] * 6,
        out_specs=(vm, vm, vm),
        scratch_shapes=[
            pltpu.VMEM(state.shape, BF16),
            pltpu.VMEM(state.shape, BF16),
            pltpu.VMEM(collision.shape, BF16),
            pltpu.VMEM((YB, VL * SLAB, LANES), F32),
            pltpu.VMEM((NB + 2 * YB, VL, LANES), BF16),
            pltpu.VMEM((NB + 2 * YB, VL, LANES), BF16),
            *[blocks] * 7,
            *[full] * 4,
            pltpu.VMEM((LANES, 2048), BF16),
            pltpu.VMEM((3, VL, LANES), F32),
            pltpu.VMEM((3, VL, LANES), F32),
            pltpu.SemaphoreType.DMA((3,)),
            pltpu.SemaphoreType.DMA((4,)),
            pltpu.SemaphoreType.DMA((4,)),
            pltpu.SemaphoreType.DMA((2,)),
            pltpu.SemaphoreType.DMA((2,)),
        ],
        compiler_params=pltpu.CompilerParams(
            collective_id=0, has_side_effects=True, vmem_limit_bytes=56 * 1024 * 1024
        ),
    )(
        state, cotangent, collision, wall_shape.reshape(16, LANES), flux_weight.reshape(16, LANES),
        courant, upwind_bits, accommodation, wall_flags,
    )


def solution(mesh):
    return jax.shard_map(
        body,
        mesh=mesh,
        in_specs=(
            P("vert", "sa", None),
            P("vert", "sa", None),
            P(),
            P(),
            P(),
            P(None, "vert"),
            P(None, "vert"),
            P(("vert", "sa"), None),
            P(("vert", "sa"), None),
        ),
        out_specs=(P("vert", "sa", None), P("vert", "sa", None), P(("vert", "sa"), None)),
        check_vma=False,
    )
```

```python
import jax
import jax.numpy as jnp
from jax import lax
from jax.experimental import pallas as pl
from jax.experimental.pallas import tpu as pltpu
from jax.sharding import PartitionSpec as P

MESH = pl.DeviceIdType.MESH
F32 = jnp.float32
BF16 = jnp.bfloat16
NZ = 32
LANES = 128
VL = 16
SLAB = 16
YB = 8
NB = SLAB * YB
TILE = 256
PER = TILE // VL
NT = 2048 // TILE
FAR_COLUMNS = ((1, 2), (1, 3), (1, 1), (1, 0), (0, 2), (0, 3), (0, 1), (0, 0))


def column(row, n):
    r = lax.broadcasted_iota(jnp.int32, (n, n), 0)
    c = lax.broadcasted_iota(jnp.int32, (n, n), 1)
    one = jnp.sum(jnp.where(r == c, jnp.broadcast_to(row, (n, n)), 0.0), axis=1, keepdims=True)
    return jnp.broadcast_to(one, (n, LANES))


def step_kernel(
    state_ref, cot_ref, coll_ref, shape_hbm, flux_hbm, cour_hbm, bits_hbm, acc_hbm, flag_hbm,
    adv_ref, prev_ref, sens_ref,
    shape_ref, flux_ref, cour_ref, bits_ref, acc_ref, flag_ref,
    svm, cvm, cmat, turn, halo_s, halo_g,
    cot_s, pas_s, adj_s, adv_s, cot_r, pas_r, adv_r,
    ws, wf, hbuf, xbuf, rt, coef, masks,
    load_sem, send_sem, recv_sem, face_ss, face_rs,
):
    me = lax.axis_index("vert")
    sa = lax.axis_index("sa")
    my_y, my_x, my_z, my_core = me // 64, (me // PER) % 4, (me // 2) % 8, me % 2
    my_column = [(my_y + dy) % 2 * 4 + (my_x + dx) % 4 for dy, dx in FAR_COLUMNS]
    my_cores = [(my_core + 1) % 2, my_core]
    near = [c * PER + core for c in my_column for core in my_cores]

    loads = [
        pltpu.make_async_copy(cot_ref, cvm, load_sem.at[0]),
        pltpu.make_async_copy(state_ref, svm, load_sem.at[1]),
        pltpu.make_async_copy(coll_ref, cmat, load_sem.at[2]),
    ]
    small = (
        (shape_hbm, shape_ref), (flux_hbm, flux_ref), (cour_hbm, cour_ref),
        (bits_hbm, bits_ref), (acc_hbm, acc_ref), (flag_hbm, flag_ref),
    )
    loads += [pltpu.make_async_copy(src, dst, load_sem.at[3 + i]) for i, (src, dst) in enumerate(small)]
    for c in loads:
        c.start()

    barrier = pltpu.get_barrier_semaphore()

    def far_z(i):
        return (my_z + 4 + i // 2 - (i % 2) * i) % 8

    def each_peer(visit):
        def place(i, _):
            z2 = far_z(i) * 2
            for n in near[:-1]:
                visit(z2 + n)

            @pl.when(i < 7)
            def _():
                visit(z2 + near[-1])

            return 0

        lax.fori_loop(0, 8, place, 0)

    def greet(d):
        pl.semaphore_signal(barrier, inc=1, device_id={"vert": d}, device_id_type=MESH)

    each_peer(greet)
    pl.semaphore_signal(barrier, inc=1, device_id={"sa": 1 - sa}, device_id_type=MESH)
    for c in loads[3:]:
        c.wait()

    for d in range(3):
        coef[d] = column(cour_ref[d : d + 1, :], VL)
        masks[d] = column(bits_ref[d : d + 1, :].astype(F32), VL)
    zero_plane = jnp.zeros((YB, VL, LANES), BF16)
    lone = sa * (NB + YB)
    halo_s[pl.ds(lone, YB)] = zero_plane
    halo_g[pl.ds(lone, YB)] = zero_plane

    def to_blocks(src, dst, base):
        def rows_in(v, _):
            plane = src[v].astype(F32)
            for j in range(YB):
                turn[j, pl.ds(v, SLAB, stride=VL), :] = plane[:, j * LANES : (j + 1) * LANES]
            return 0

        lax.fori_loop(0, VL, rows_in, 0, unroll=4)

        def planes_out(x, _):
            for j in range(YB):
                part = turn[j, pl.ds(pl.multiple_of(x * VL, VL), VL), :]
                dst[base + x * YB + j] = part.astype(BF16)
            return 0

        lax.fori_loop(0, SLAB, planes_out, 0, unroll=2)

    def send(src, src_base, dst, dst_base, phase, d):
        pltpu.make_async_remote_copy(
            src_ref=src.at[src_base + d],
            dst_ref=dst.at[dst_base + me],
            send_sem=send_sem.at[phase],
            recv_sem=recv_sem.at[phase],
            device_id={"vert": d},
            device_id_type=MESH,
        ).start()

    def column_of(k):
        dx = 2 + k % 4 - (k % 4 // 2) * (2 * (k % 4) - 1)
        return (my_y + 1 - k // 4) % 2 * 4 + (my_x + dx) % 4

    def send_column(src, dst, phase, k):
        first = column_of(k) * PER

        def place(i, _):
            z2 = far_z(i) * 2 + first
            send(src, 0, dst, 0, phase, z2 + my_cores[0])

            @pl.when(i + k < 14)
            def _():
                send(src, 0, dst, 0, phase, z2 + my_cores[1])

            return 0

        lax.fori_loop(0, 8, place, 0)

    def send_all(src, src_base, dst, dst_base, phase):
        each_peer(lambda d: send(src, src_base, dst, dst_base, phase, d))

    def wait_blocks(ref, sem):
        part = ref.at[pl.ds(0, NB - 1)]
        pltpu.make_async_copy(part, part, sem).wait()

    def face(buf, k):
        return pltpu.make_async_remote_copy(
            src_ref=buf.at[pl.ds(YB + (NB - YB) * (1 - sa), YB)],
            dst_ref=buf.at[pl.ds((NB + YB) * sa, YB)],
            send_sem=face_ss.at[k],
            recv_sem=face_rs.at[k],
            device_id={"sa": 1 - sa},
            device_id_type=MESH,
        )

    lane = lax.broadcasted_iota(jnp.int32, (VL, LANES), 1)
    z_at = lane % NZ

    def transport(buf, forward, emit):
        def plane(x, _):
            base = x * YB
            mid = [buf[base + YB + j].astype(F32) for j in range(YB)]
            up32 = [pltpu.roll(m, NZ, 1) for m in mid]
            dn32 = [pltpu.roll(m, LANES - NZ, 1) for m in mid]
            zero = jnp.zeros((VL, LANES), F32)
            for j in range(YB):
                m = mid[j]
                minus = (
                    buf[base + j].astype(F32),
                    jnp.where(lane < NZ, up32[j - 1] if j else zero, up32[j]),
                    jnp.where(z_at != 0, pltpu.roll(m, 1, 1), 0.0),
                )
                plus = (
                    buf[base + 2 * YB + j].astype(F32),
                    jnp.where(lane >= LANES - NZ, dn32[j + 1] if j < YB - 1 else zero, dn32[j]),
                    jnp.where(z_at != NZ - 1, pltpu.roll(m, LANES - 1, 1), 0.0),
                )
                res = m
                for d in range(3):
                    up = masks[d] == 1.0
                    donor = jnp.where(up, minus[d], plus[d]) if forward else jnp.where(up, plus[d], minus[d])
                    res = res - coef[d] * (m - donor)
                emit(x, j, res)
            return 0

        lax.fori_loop(0, SLAB, plane, 0)

    def out_rows(dst):
        def one(v, _):
            for j in range(YB):
                rows = turn[j, pl.ds(pl.multiple_of(v * SLAB, SLAB), SLAB), :]
                dst[v, :, j * LANES : (j + 1) * LANES] = rows.astype(BF16)
            return 0

        lax.fori_loop(0, VL, one, 0, unroll=2)

    loads[0].wait()
    to_blocks(cvm, cot_s, 0)
    loads[1].wait()
    to_blocks(svm, halo_s, YB)

    pl.semaphore_wait(barrier, NB)
    face_s = face(halo_s, 0)
    face_s.start()
    send_all(cot_s, 0, cot_r, 0, 0)
    cot_r[me] = cot_s[me]

    face_s.wait()

    def emit_passed(x, j, res):
        pas_s[x * YB + j] = res.astype(BF16)

    transport(halo_s, True, emit_passed)
    send_all(pas_s, 0, pas_r, 0, 1)
    pas_r[me] = pas_s[me]

    def spread(g, _):
        rows = pl.ds(pl.multiple_of(g * LANES, LANES), LANES)
        ws[rows, :] = jnp.broadcast_to(shape_ref[pl.ds(g, 1), :], (LANES, LANES)).T
        wf[rows, :] = jnp.broadcast_to(flux_ref[pl.ds(g, 1), :], (LANES, LANES)).T
        return 0

    lax.fori_loop(0, 2048 // LANES, spread, 0)
    flags = flag_ref[...].astype(F32)
    gain = acc_ref[...] * flags

    def tile_rows(t):
        return pl.ds(pl.multiple_of(t * TILE, TILE), TILE)

    def tile_blocks(t):
        return pl.ds(pl.multiple_of(t * PER, PER), PER)

    def fold(a):
        return jnp.sum(a.reshape(TILE // 8, 8, LANES), axis=0)

    loads[2].wait()
    wait_blocks(cot_r, recv_sem.at[0])
    cot_all = cot_r.reshape(2048, LANES)

    def adjoint_tile(t, total):
        rows = tile_rows(t)
        h = jnp.dot(cmat[rows, :], cot_all[...], preferred_element_type=F32)
        h = cot_all[rows, :].astype(F32) + h
        hbuf[rows, :] = h
        return total + fold(ws[rows, :] * h)

    total = lax.fori_loop(0, NT, adjoint_tile, jnp.zeros((8, LANES), F32))
    weighted = jnp.sum(total, axis=0, keepdims=True)

    def adjoint_out(k, _):
        rows = tile_rows(k)
        h = hbuf[rows, :]
        g = h + gain * (wf[rows, :] * weighted - h)
        adj_s[tile_blocks(k)] = g.astype(BF16).reshape(PER, VL, LANES)
        return 0

    lax.fori_loop(0, NT, adjoint_out, 0)
    send_all(adj_s, 0, halo_g, YB, 2)
    halo_g[YB + me] = adj_s[me]

    wait_blocks(pas_r, recv_sem.at[1])
    pas_all = pas_r.reshape(2048, LANES)

    def density_tile(t, total):
        rows = tile_rows(t)
        return total + fold(wf[rows, :] * pas_all[rows, :].astype(F32))

    total = lax.fori_loop(0, NT, density_tile, jnp.zeros((8, LANES), F32))
    density = jnp.sum(total, axis=0, keepdims=True)

    def relax_block(g, total):
        rows = pl.ds(pl.multiple_of(g * LANES, LANES), LANES)
        moved = pas_all[rows, :].astype(F32)
        target = ws[rows, :] * density - moved
        relaxed = moved + gain * target
        xbuf[rows, :] = relaxed
        rt[:, rows] = relaxed.T.astype(BF16)
        return total + jnp.sum((hbuf[rows, :] * target).reshape(LANES // 8, 8, LANES), axis=0)

    total = lax.fori_loop(0, 2048 // LANES, relax_block, jnp.zeros((8, LANES), F32))
    sens_ref[...] = flags * jnp.sum(total, axis=0, keepdims=True)

    def forward_tile(k, _):
        t = column_of(k)
        rows = tile_rows(t)
        mixed = jnp.dot(rt[...], cmat[:, rows], preferred_element_type=F32)
        adv = xbuf[rows, :] + mixed.T
        adv_s[tile_blocks(t)] = adv.astype(BF16).reshape(PER, VL, LANES)

        @pl.when(k > 0)
        def _():
            send_column(adv_s, adv_r, 3, k - 1)

        return 0

    lax.fori_loop(0, NT, forward_tile, 0)
    send_column(adv_s, adv_r, 3, NT - 1)
    adv_r[me] = adv_s[me]

    wait_blocks(halo_g, recv_sem.at[2])
    face_g = face(halo_g, 1)
    face_g.start()
    face_g.wait()

    def emit_previous(x, j, res):
        turn[j, pl.ds(x, VL, stride=SLAB), :] = res

    transport(halo_g, False, emit_previous)
    out_rows(prev_ref)

    wait_blocks(adv_r, recv_sem.at[3])

    def unpack(x, _):
        for j in range(YB):
            turn[j, pl.ds(x, VL, stride=SLAB), :] = adv_r[x * YB + j].astype(F32)
        return 0

    lax.fori_loop(0, SLAB, unpack, 0, unroll=2)
    out_rows(adv_ref)

    for phase, buf in enumerate((cot_s, pas_s, adj_s, adv_s)):
        wait_blocks(buf, send_sem.at[phase])


def write_kernel(a_ref, b_ref, c_ref, a_out, b_out, c_out, sems):
    pairs = ((a_ref, a_out), (b_ref, b_out), (c_ref, c_out))
    copies = [pltpu.make_async_copy(src, dst, sems.at[i]) for i, (src, dst) in enumerate(pairs)]
    for c in copies:
        c.start()
    for c in copies:
        c.wait()


def body(state, cotangent, collision, wall_shape, flux_weight, courant, upwind_bits, accommodation, wall_flags):
    vm = pl.BlockSpec(memory_space=pltpu.VMEM)
    hb = pl.BlockSpec(memory_space=pltpu.HBM)
    blocks = pltpu.VMEM((NB, VL, LANES), BF16)
    full = pltpu.VMEM((2048, LANES), F32)
    results = pl.pallas_call(
        step_kernel,
        name="step",
        out_shape=(
            jax.ShapeDtypeStruct(state.shape, BF16),
            jax.ShapeDtypeStruct(state.shape, BF16),
            jax.ShapeDtypeStruct(accommodation.shape, F32),
        ),
        in_specs=[hb] * 9,
        out_specs=(vm, vm, vm),
        scratch_shapes=[
            pltpu.VMEM((16, LANES), F32),
            pltpu.VMEM((16, LANES), F32),
            pltpu.VMEM(courant.shape, F32),
            pltpu.VMEM(upwind_bits.shape, jnp.int32),
            pltpu.VMEM(accommodation.shape, F32),
            pltpu.VMEM(wall_flags.shape, jnp.int32),
            pltpu.VMEM(state.shape, BF16),
            pltpu.VMEM(state.shape, BF16),
            pltpu.VMEM(collision.shape, BF16),
            pltpu.VMEM((YB, VL * SLAB, LANES), F32),
            pltpu.VMEM((NB + 2 * YB, VL, LANES), BF16),
            pltpu.VMEM((NB + 2 * YB, VL, LANES), BF16),
            *[blocks] * 7,
            *[full] * 4,
            pltpu.VMEM((LANES, 2048), BF16),
            pltpu.VMEM((3, VL, LANES), F32),
            pltpu.VMEM((3, VL, LANES), F32),
            pltpu.SemaphoreType.DMA((9,)),
            pltpu.SemaphoreType.DMA((4,)),
            pltpu.SemaphoreType.DMA((4,)),
            pltpu.SemaphoreType.DMA((2,)),
            pltpu.SemaphoreType.DMA((2,)),
        ],
        compiler_params=pltpu.CompilerParams(
            collective_id=0, has_side_effects=True, vmem_limit_bytes=55312384
        ),
    )(
        state, cotangent, collision, wall_shape.reshape(16, LANES), flux_weight.reshape(16, LANES),
        courant, upwind_bits, accommodation, wall_flags,
    )
    return pl.pallas_call(
        write_kernel,
        name="write",
        out_shape=tuple(jax.ShapeDtypeStruct(r.shape, r.dtype) for r in results),
        in_specs=[vm] * 3,
        out_specs=(hb, hb, hb),
        scratch_shapes=[pltpu.SemaphoreType.DMA((3,))],
        compiler_params=pltpu.CompilerParams(vmem_limit_bytes=1024 * 1024),
    )(*results)


def solution(mesh):
    return jax.shard_map(
        body,
        mesh=mesh,
        in_specs=(
            P("vert", "sa", None),
            P("vert", "sa", None),
            P(),
            P(),
            P(),
            P(None, "vert"),
            P(None, "vert"),
            P(("vert", "sa"), None),
            P(("vert", "sa"), None),
        ),
        out_specs=(P("vert", "sa", None), P("vert", "sa", None), P(("vert", "sa"), None)),
        check_vma=False,
    )
```

```python
import jax
import jax.numpy as jnp
from jax import lax
from jax.experimental import pallas as pl
from jax.experimental.pallas import tpu as pltpu
from jax.sharding import PartitionSpec as P

MESH = pl.DeviceIdType.MESH
F32 = jnp.float32
BF16 = jnp.bfloat16
NZ = 32
LANES = 128
VL = 16
SLAB = 16
YB = 8
NB = SLAB * YB
TILE = 256
PER = TILE // VL
NT = 2048 // TILE
FAR_COLUMNS = ((1, 2), (1, 3), (1, 1), (1, 0), (0, 2), (0, 3), (0, 1), (0, 0))


def column(row, n):
    r = lax.broadcasted_iota(jnp.int32, (n, n), 0)
    c = lax.broadcasted_iota(jnp.int32, (n, n), 1)
    one = jnp.sum(jnp.where(r == c, jnp.broadcast_to(row, (n, n)), 0.0), axis=1, keepdims=True)
    return jnp.broadcast_to(one, (n, LANES))


def step_kernel(
    state_ref, cot_ref, coll_ref, shape_hbm, flux_hbm, cour_hbm, bits_hbm, acc_hbm, flag_hbm,
    adv_ref, prev_ref, sens_ref,
    shape_ref, flux_ref, cour_ref, bits_ref, acc_ref, flag_ref,
    svm, cvm, cmat, turn, halo_s, halo_g,
    cot_s, pas_s, adj_s, adv_s, cot_r, pas_r, adv_r,
    ws, wf, hbuf, xbuf, rt, coef, masks,
    load_sem, send_sem, recv_sem, face_ss, face_rs,
):
    me = lax.axis_index("vert")
    sa = lax.axis_index("sa")
    my_y, my_x, my_z, my_core = me // 64, (me // PER) % 4, (me // 2) % 8, me % 2
    my_column = [(my_y + dy) % 2 * 4 + (my_x + dx) % 4 for dy, dx in FAR_COLUMNS]
    my_cores = [(my_core + 1) % 2, my_core]
    near = [c * PER + core for c in my_column for core in my_cores]

    loads = [
        pltpu.make_async_copy(cot_ref, cvm, load_sem.at[0]),
        pltpu.make_async_copy(state_ref, svm, load_sem.at[1]),
        pltpu.make_async_copy(coll_ref, cmat, load_sem.at[2]),
    ]
    small = (
        (shape_hbm, shape_ref), (flux_hbm, flux_ref), (cour_hbm, cour_ref),
        (bits_hbm, bits_ref), (acc_hbm, acc_ref), (flag_hbm, flag_ref),
    )
    loads += [pltpu.make_async_copy(src, dst, load_sem.at[3 + i]) for i, (src, dst) in enumerate(small)]
    for c in loads:
        c.start()

    barrier = pltpu.get_barrier_semaphore()

    def far_z(i):
        return (my_z + 4 + i // 2 - (i % 2) * i) % 8

    def each_peer(visit):
        def place(i, _):
            z2 = far_z(i) * 2
            for n in near[:-1]:
                visit(z2 + n)

            @pl.when(i < 7)
            def _():
                visit(z2 + near[-1])

            return 0

        lax.fori_loop(0, 8, place, 0)

    def greet(d):
        pl.semaphore_signal(barrier, inc=1, device_id={"vert": d}, device_id_type=MESH)

    each_peer(greet)
    pl.semaphore_signal(barrier, inc=1, device_id={"sa": 1 - sa}, device_id_type=MESH)
    for c in loads[3:]:
        c.wait()

    for d in range(3):
        coef[d] = column(cour_ref[d : d + 1, :], VL)
        masks[d] = column(bits_ref[d : d + 1, :].astype(F32), VL)
    zero_plane = jnp.zeros((YB, VL, LANES), BF16)
    lone = sa * (NB + YB)
    halo_s[pl.ds(lone, YB)] = zero_plane
    halo_g[pl.ds(lone, YB)] = zero_plane

    def to_blocks(src, dst, base):
        def rows_in(v, _):
            plane = src[v].astype(F32)
            for j in range(YB):
                turn[j, pl.ds(v, SLAB, stride=VL), :] = plane[:, j * LANES : (j + 1) * LANES]
            return 0

        lax.fori_loop(0, VL, rows_in, 0, unroll=4)

        def planes_out(x, _):
            for j in range(YB):
                part = turn[j, pl.ds(pl.multiple_of(x * VL, VL), VL), :]
                dst[base + x * YB + j] = part.astype(BF16)
            return 0

        lax.fori_loop(0, SLAB, planes_out, 0, unroll=2)

    def send(src, src_base, dst, dst_base, phase, d):
        pltpu.make_async_remote_copy(
            src_ref=src.at[src_base + d],
            dst_ref=dst.at[dst_base + me],
            send_sem=send_sem.at[phase],
            recv_sem=recv_sem.at[phase],
            device_id={"vert": d},
            device_id_type=MESH,
        ).start()

    def column_of(k):
        dx = 2 + k % 4 - (k % 4 // 2) * (2 * (k % 4) - 1)
        return (my_y + 1 - k // 4) % 2 * 4 + (my_x + dx) % 4

    def send_column(src, dst, phase, k):
        first = column_of(k) * PER

        def place(i, _):
            z2 = far_z(i) * 2 + first
            send(src, 0, dst, 0, phase, z2 + my_cores[0])

            @pl.when(i + k < 14)
            def _():
                send(src, 0, dst, 0, phase, z2 + my_cores[1])

            return 0

        lax.fori_loop(0, 8, place, 0)

    def send_all(src, src_base, dst, dst_base, phase):
        each_peer(lambda d: send(src, src_base, dst, dst_base, phase, d))

    def wait_blocks(ref, sem):
        part = ref.at[pl.ds(0, NB - 1)]
        pltpu.make_async_copy(part, part, sem).wait()

    def face(buf, k):
        return pltpu.make_async_remote_copy(
            src_ref=buf.at[pl.ds(YB + (NB - YB) * (1 - sa), YB)],
            dst_ref=buf.at[pl.ds((NB + YB) * sa, YB)],
            send_sem=face_ss.at[k],
            recv_sem=face_rs.at[k],
            device_id={"sa": 1 - sa},
            device_id_type=MESH,
        )

    lane = lax.broadcasted_iota(jnp.int32, (VL, LANES), 1)
    z_at = lane % NZ

    def transport(buf, forward, emit):
        def plane(x, _):
            base = x * YB
            mid = [buf[base + YB + j].astype(F32) for j in range(YB)]
            up32 = [pltpu.roll(m, NZ, 1) for m in mid]
            dn32 = [pltpu.roll(m, LANES - NZ, 1) for m in mid]
            zero = jnp.zeros((VL, LANES), F32)
            for j in range(YB):
                m = mid[j]
                minus = (
                    buf[base + j].astype(F32),
                    jnp.where(lane < NZ, up32[j - 1] if j else zero, up32[j]),
                    jnp.where(z_at != 0, pltpu.roll(m, 1, 1), 0.0),
                )
                plus = (
                    buf[base + 2 * YB + j].astype(F32),
                    jnp.where(lane >= LANES - NZ, dn32[j + 1] if j < YB - 1 else zero, dn32[j]),
                    jnp.where(z_at != NZ - 1, pltpu.roll(m, LANES - 1, 1), 0.0),
                )
                res = m
                for d in range(3):
                    up = masks[d] == 1.0
                    donor = jnp.where(up, minus[d], plus[d]) if forward else jnp.where(up, plus[d], minus[d])
                    res = res - coef[d] * (m - donor)
                emit(x, j, res)
            return 0

        lax.fori_loop(0, SLAB, plane, 0)

    def out_rows(dst):
        def one(v, _):
            for j in range(YB):
                rows = turn[j, pl.ds(pl.multiple_of(v * SLAB, SLAB), SLAB), :]
                dst[v, :, j * LANES : (j + 1) * LANES] = rows.astype(BF16)
            return 0

        lax.fori_loop(0, VL, one, 0, unroll=2)

    loads[0].wait()
    to_blocks(cvm, cot_s, 0)
    loads[1].wait()
    to_blocks(svm, halo_s, YB)

    pl.semaphore_wait(barrier, NB)
    face_s = face(halo_s, 0)
    face_s.start()
    send_all(cot_s, 0, cot_r, 0, 0)
    cot_r[me] = cot_s[me]

    face_s.wait()

    def emit_passed(x, j, res):
        pas_s[x * YB + j] = res.astype(BF16)

    transport(halo_s, True, emit_passed)
    send_all(pas_s, 0, pas_r, 0, 1)
    pas_r[me] = pas_s[me]

    def spread(g, _):
        rows = pl.ds(pl.multiple_of(g * LANES, LANES), LANES)
        ws[rows, :] = jnp.broadcast_to(shape_ref[pl.ds(g, 1), :], (LANES, LANES)).T
        wf[rows, :] = jnp.broadcast_to(flux_ref[pl.ds(g, 1), :], (LANES, LANES)).T
        return 0

    lax.fori_loop(0, 2048 // LANES, spread, 0)
    flags = flag_ref[...].astype(F32)
    gain = acc_ref[...] * flags

    def tile_rows(t):
        return pl.ds(pl.multiple_of(t * TILE, TILE), TILE)

    def tile_blocks(t):
        return pl.ds(pl.multiple_of(t * PER, PER), PER)

    def fold(a):
        return jnp.sum(a.reshape(TILE // 8, 8, LANES), axis=0)

    loads[2].wait()
    wait_blocks(cot_r, recv_sem.at[0])
    cot_all = cot_r.reshape(2048, LANES)

    def adjoint_tile(t, total):
        rows = tile_rows(t)
        h = jnp.dot(cmat[rows, :], cot_all[...], preferred_element_type=F32)
        h = cot_all[rows, :].astype(F32) + h
        hbuf[rows, :] = h
        return total + fold(ws[rows, :] * h)

    total = lax.fori_loop(0, NT, adjoint_tile, jnp.zeros((8, LANES), F32))
    weighted = jnp.sum(total, axis=0, keepdims=True)

    def adjoint_out(k, _):
        rows = tile_rows(k)
        h = hbuf[rows, :]
        g = h + gain * (wf[rows, :] * weighted - h)
        adj_s[tile_blocks(k)] = g.astype(BF16).reshape(PER, VL, LANES)
        return 0

    lax.fori_loop(0, NT, adjoint_out, 0)
    send_all(adj_s, 0, halo_g, YB, 2)
    halo_g[YB + me] = adj_s[me]

    wait_blocks(pas_r, recv_sem.at[1])
    pas_all = pas_r.reshape(2048, LANES)

    def density_tile(t, total):
        rows = tile_rows(t)
        return total + fold(wf[rows, :] * pas_all[rows, :].astype(F32))

    total = lax.fori_loop(0, NT, density_tile, jnp.zeros((8, LANES), F32))
    density = jnp.sum(total, axis=0, keepdims=True)

    def relax_block(g, total):
        rows = pl.ds(pl.multiple_of(g * LANES, LANES), LANES)
        moved = pas_all[rows, :].astype(F32)
        target = ws[rows, :] * density - moved
        relaxed = moved + gain * target
        xbuf[rows, :] = relaxed
        rt[:, rows] = relaxed.T.astype(BF16)
        return total + jnp.sum((hbuf[rows, :] * target).reshape(LANES // 8, 8, LANES), axis=0)

    total = lax.fori_loop(0, 2048 // LANES, relax_block, jnp.zeros((8, LANES), F32))
    sens_ref[...] = flags * jnp.sum(total, axis=0, keepdims=True)

    def forward_tile(k, _):
        t = column_of(k)
        rows = tile_rows(t)
        mixed = jnp.dot(rt[...], cmat[:, rows], preferred_element_type=F32)
        adv = xbuf[rows, :] + mixed.T
        adv_s[tile_blocks(t)] = adv.astype(BF16).reshape(PER, VL, LANES)

        @pl.when(k > 0)
        def _():
            send_column(adv_s, adv_r, 3, k - 1)

        return 0

    lax.fori_loop(0, NT, forward_tile, 0)
    send_column(adv_s, adv_r, 3, NT - 1)
    adv_r[me] = adv_s[me]

    wait_blocks(halo_g, recv_sem.at[2])
    face_g = face(halo_g, 1)
    face_g.start()
    face_g.wait()

    def emit_previous(x, j, res):
        turn[j, pl.ds(x, VL, stride=SLAB), :] = res

    transport(halo_g, False, emit_previous)
    out_rows(prev_ref)

    wait_blocks(adv_r, recv_sem.at[3])

    def unpack(x, _):
        for j in range(YB):
            turn[j, pl.ds(x, VL, stride=SLAB), :] = adv_r[x * YB + j].astype(F32)
        return 0

    lax.fori_loop(0, SLAB, unpack, 0, unroll=2)
    out_rows(adv_ref)

    for phase, buf in enumerate((cot_s, pas_s, adj_s, adv_s)):
        wait_blocks(buf, send_sem.at[phase])


def write_kernel(a_ref, b_ref, c_ref, a_out, b_out, c_out, sems):
    pairs = ((a_ref, a_out), (b_ref, b_out), (c_ref, c_out))
    copies = [pltpu.make_async_copy(src, dst, sems.at[i]) for i, (src, dst) in enumerate(pairs)]
    for c in copies:
        c.start()
    for c in copies:
        c.wait()


def body(state, cotangent, collision, wall_shape, flux_weight, courant, upwind_bits, accommodation, wall_flags):
    vm = pl.BlockSpec(memory_space=pltpu.VMEM)
    hb = pl.BlockSpec(memory_space=pltpu.HBM)
    blocks = pltpu.VMEM((NB, VL, LANES), BF16)
    full = pltpu.VMEM((2048, LANES), F32)
    results = pl.pallas_call(
        step_kernel,
        name="step",
        out_shape=(
            jax.ShapeDtypeStruct(state.shape, BF16),
            jax.ShapeDtypeStruct(state.shape, BF16),
            jax.ShapeDtypeStruct(accommodation.shape, F32),
        ),
        in_specs=[hb] * 9,
        out_specs=(vm, vm, vm),
        scratch_shapes=[
            pltpu.VMEM((16, LANES), F32),
            pltpu.VMEM((16, LANES), F32),
            pltpu.VMEM(courant.shape, F32),
            pltpu.VMEM(upwind_bits.shape, jnp.int32),
            pltpu.VMEM(accommodation.shape, F32),
            pltpu.VMEM(wall_flags.shape, jnp.int32),
            pltpu.VMEM(state.shape, BF16),
            pltpu.VMEM(state.shape, BF16),
            pltpu.VMEM(collision.shape, BF16),
            pltpu.VMEM((YB, VL * SLAB, LANES), F32),
            pltpu.VMEM((NB + 2 * YB, VL, LANES), BF16),
            pltpu.VMEM((NB + 2 * YB, VL, LANES), BF16),
            *[blocks] * 7,
            *[full] * 4,
            pltpu.VMEM((LANES, 2048), BF16),
            pltpu.VMEM((3, VL, LANES), F32),
            pltpu.VMEM((3, VL, LANES), F32),
            pltpu.SemaphoreType.DMA((9,)),
            pltpu.SemaphoreType.DMA((4,)),
            pltpu.SemaphoreType.DMA((4,)),
            pltpu.SemaphoreType.DMA((2,)),
            pltpu.SemaphoreType.DMA((2,)),
        ],
        compiler_params=pltpu.CompilerParams(
            collective_id=0, has_side_effects=True, vmem_limit_bytes=32 * 1024 * 1024
        ),
    )(
        *[
            pltpu.with_memory_space_constraint(a, pltpu.HBM)
            for a in (
                state, cotangent, collision, wall_shape.reshape(16, LANES), flux_weight.reshape(16, LANES),
                courant, upwind_bits, accommodation, wall_flags,
            )
        ]
    )
    return pl.pallas_call(
        write_kernel,
        name="write",
        out_shape=tuple(jax.ShapeDtypeStruct(r.shape, r.dtype) for r in results),
        in_specs=[vm] * 3,
        out_specs=(hb, hb, hb),
        scratch_shapes=[pltpu.SemaphoreType.DMA((3,))],
        compiler_params=pltpu.CompilerParams(vmem_limit_bytes=1024 * 1024),
    )(*results)


def solution(mesh):
    return jax.shard_map(
        body,
        mesh=mesh,
        in_specs=(
            P("vert", "sa", None),
            P("vert", "sa", None),
            P(),
            P(),
            P(),
            P(None, "vert"),
            P(None, "vert"),
            P(("vert", "sa"), None),
            P(("vert", "sa"), None),
        ),
        out_specs=(P("vert", "sa", None), P("vert", "sa", None), P(("vert", "sa"), None)),
        check_vma=False,
    )
```

```python
import jax
import jax.numpy as jnp
from jax import lax
from jax.experimental import pallas as pl
from jax.experimental.pallas import tpu as pltpu
from jax.sharding import PartitionSpec as P

MESH = pl.DeviceIdType.MESH
F32 = jnp.float32
BF16 = jnp.bfloat16
NZ = 32
LANES = 128
VL = 16
SLAB = 16
YB = 8
NB = SLAB * YB
TILE = 256
PER = TILE // VL
NT = 2048 // TILE
FAR_COLUMNS = ((1, 2), (1, 3), (1, 1), (1, 0), (0, 2), (0, 3), (0, 1), (0, 0))


def column(row, n):
    r = lax.broadcasted_iota(jnp.int32, (n, n), 0)
    c = lax.broadcasted_iota(jnp.int32, (n, n), 1)
    one = jnp.sum(jnp.where(r == c, jnp.broadcast_to(row, (n, n)), 0.0), axis=1, keepdims=True)
    return jnp.broadcast_to(one, (n, LANES))


def step_kernel(
    state_ref, cot_ref, coll_ref, shape_hbm, flux_hbm, cour_hbm, bits_hbm, acc_hbm, flag_hbm,
    adv_ref, prev_ref, sens_ref,
    shape_ref, flux_ref, cour_ref, bits_ref, acc_ref, flag_ref,
    svm, cvm, cmat, turn, halo_s, halo_g,
    cot_s, pas_s, adj_s, adv_s, cot_r, pas_r, adv_r,
    ws, wf, hbuf, xbuf, rt, coef, masks,
    load_sem, send_sem, recv_sem, face_ss, face_rs, line_ss, line_rs, cot_relay, pas_relay,
):
    me = lax.axis_index("vert")
    sa = lax.axis_index("sa")
    my_y, my_x, my_z, my_core = me // 64, (me // PER) % 4, (me // 2) % 8, me % 2
    my_column = [(my_y + dy) % 2 * 4 + (my_x + dx) % 4 for dy, dx in FAR_COLUMNS]
    my_cores = [(my_core + 1) % 2, my_core]
    near = [c * PER + core for c in my_column for core in my_cores]

    loads = [
        pltpu.make_async_copy(cot_ref, cvm, load_sem.at[0]),
        pltpu.make_async_copy(state_ref, svm, load_sem.at[1]),
        pltpu.make_async_copy(coll_ref, cmat, load_sem.at[2]),
    ]
    small = (
        (shape_hbm, shape_ref), (flux_hbm, flux_ref), (cour_hbm, cour_ref),
        (bits_hbm, bits_ref), (acc_hbm, acc_ref), (flag_hbm, flag_ref),
    )
    loads += [pltpu.make_async_copy(src, dst, load_sem.at[3 + i]) for i, (src, dst) in enumerate(small)]
    for c in loads:
        c.start()

    barrier = pltpu.get_barrier_semaphore()

    def far_z(i):
        return (my_z + 4 + i // 2 - (i % 2) * i) % 8

    def each_peer(visit):
        def place(i, _):
            z2 = far_z(i) * 2
            for n in near[:-1]:
                visit(z2 + n)

            @pl.when(i < 7)
            def _():
                visit(z2 + near[-1])

            return 0

        lax.fori_loop(0, 8, place, 0)

    def greet(d):
        pl.semaphore_signal(barrier, inc=1, device_id={"vert": d}, device_id_type=MESH)

    my_col = my_y * 4 + my_x
    for i in range(7):
        greet(my_col * PER + far_z(i) * 2 + my_core)
    for n in near[:-1]:
        greet(n + my_z * 2)
    pl.semaphore_signal(barrier, inc=1, device_id={"sa": 1 - sa}, device_id_type=MESH)
    for c in loads[3:]:
        c.wait()

    for d in range(3):
        coef[d] = column(cour_ref[d : d + 1, :], VL)
        masks[d] = column(bits_ref[d : d + 1, :].astype(F32), VL)
    zero_plane = jnp.zeros((YB, VL, LANES), BF16)
    lone = sa * (NB + YB)
    halo_s[pl.ds(lone, YB)] = zero_plane
    halo_g[pl.ds(lone, YB)] = zero_plane

    def to_blocks(src, dst, base):
        def rows_in(v, _):
            plane = src[v].astype(F32)
            for j in range(YB):
                turn[j, pl.ds(v, SLAB, stride=VL), :] = plane[:, j * LANES : (j + 1) * LANES]
            return 0

        lax.fori_loop(0, VL, rows_in, 0, unroll=4)

        def planes_out(x, _):
            for j in range(YB):
                part = turn[j, pl.ds(pl.multiple_of(x * VL, VL), VL), :]
                dst[base + x * YB + j] = part.astype(BF16)
            return 0

        lax.fori_loop(0, SLAB, planes_out, 0, unroll=2)

    def send(src, src_base, dst, dst_base, phase, d):
        pltpu.make_async_remote_copy(
            src_ref=src.at[src_base + d],
            dst_ref=dst.at[dst_base + me],
            send_sem=send_sem.at[phase],
            recv_sem=recv_sem.at[phase],
            device_id={"vert": d},
            device_id_type=MESH,
        ).start()

    def column_of(k):
        dx = 2 + k % 4 - (k % 4 // 2) * (2 * (k % 4) - 1)
        return (my_y + 1 - k // 4) % 2 * 4 + (my_x + dx) % 4

    def send_column(src, dst, phase, k):
        first = column_of(k) * PER

        def place(i, _):
            z2 = far_z(i) * 2 + first
            send(src, 0, dst, 0, phase, z2 + my_cores[0])

            @pl.when(i + k < 14)
            def _():
                send(src, 0, dst, 0, phase, z2 + my_cores[1])

            return 0

        lax.fori_loop(0, 8, place, 0)

    def send_all(src, src_base, dst, dst_base, phase):
        each_peer(lambda d: send(src, src_base, dst, dst_base, phase, d))

    def by_place(ref):
        return ref.reshape(8, 8, 2, VL, LANES)

    def send_line(src, relay, k):
        def place(i, _):
            z = far_z(i)
            pltpu.make_async_remote_copy(
                src_ref=by_place(src).at[:, z],
                dst_ref=relay.at[my_z],
                send_sem=line_ss.at[k],
                recv_sem=line_rs.at[k, my_z],
                device_id={"vert": my_col * PER + z * 2 + my_core},
                device_id_type=MESH,
            ).start()
            return 0

        lax.fori_loop(0, 7, place, 0)

    def send_plane(part, dst, k, z):
        for col in my_column:
            for core in my_cores:
                if col is my_column[-1] and core is my_cores[-1]:
                    continue
                pltpu.make_async_remote_copy(
                    src_ref=part.at[col, core],
                    dst_ref=by_place(dst).at[my_col, z, my_core],
                    send_sem=send_sem.at[k],
                    recv_sem=recv_sem.at[k],
                    device_id={"vert": (col * 8 + my_z) * 2 + core},
                    device_id_type=MESH,
                ).start()
        dst[(my_col * 8 + z) * 2 + my_core] = part[my_col, my_core]

    def start_exchange(src, relay, dst, k):
        send_line(src, relay, k)
        send_plane(by_place(src).at[:, my_z], dst, k, my_z)

    def relay_exchange(relay, dst, k):
        def place(i, _):
            z = far_z(i)
            part = relay.at[z]
            pltpu.make_async_copy(part, part, line_rs.at[k, z]).wait()
            send_plane(part, dst, k, z)
            return 0

        lax.fori_loop(0, 7, place, 0)

    def wait_blocks(ref, sem, blocks=NB - 1):
        part = ref.at[pl.ds(0, blocks)]
        pltpu.make_async_copy(part, part, sem).wait()

    def face(buf, k):
        return pltpu.make_async_remote_copy(
            src_ref=buf.at[pl.ds(YB + (NB - YB) * (1 - sa), YB)],
            dst_ref=buf.at[pl.ds((NB + YB) * sa, YB)],
            send_sem=face_ss.at[k],
            recv_sem=face_rs.at[k],
            device_id={"sa": 1 - sa},
            device_id_type=MESH,
        )

    lane = lax.broadcasted_iota(jnp.int32, (VL, LANES), 1)
    z_at = lane % NZ

    def transport(buf, forward, emit):
        def plane(x, _):
            base = x * YB
            mid = [buf[base + YB + j].astype(F32) for j in range(YB)]
            up32 = [pltpu.roll(m, NZ, 1) for m in mid]
            dn32 = [pltpu.roll(m, LANES - NZ, 1) for m in mid]
            zero = jnp.zeros((VL, LANES), F32)
            for j in range(YB):
                m = mid[j]
                minus = (
                    buf[base + j].astype(F32),
                    jnp.where(lane < NZ, up32[j - 1] if j else zero, up32[j]),
                    jnp.where(z_at != 0, pltpu.roll(m, 1, 1), 0.0),
                )
                plus = (
                    buf[base + 2 * YB + j].astype(F32),
                    jnp.where(lane >= LANES - NZ, dn32[j + 1] if j < YB - 1 else zero, dn32[j]),
                    jnp.where(z_at != NZ - 1, pltpu.roll(m, LANES - 1, 1), 0.0),
                )
                res = m
                for d in range(3):
                    up = masks[d] == 1.0
                    donor = jnp.where(up, minus[d], plus[d]) if forward else jnp.where(up, plus[d], minus[d])
                    res = res - coef[d] * (m - donor)
                emit(x, j, res)
            return 0

        lax.fori_loop(0, SLAB, plane, 0)

    def out_rows(dst):
        def one(v, _):
            for j in range(YB):
                rows = turn[j, pl.ds(pl.multiple_of(v * SLAB, SLAB), SLAB), :]
                dst[v, :, j * LANES : (j + 1) * LANES] = rows.astype(BF16)
            return 0

        lax.fori_loop(0, VL, one, 0, unroll=2)

    loads[0].wait()
    to_blocks(cvm, cot_s, 0)
    pl.semaphore_wait(barrier, 23)
    start_exchange(cot_s, cot_relay, cot_r, 0)
    loads[1].wait()
    to_blocks(svm, halo_s, YB)
    face_s = face(halo_s, 0)
    face_s.start()

    face_s.wait()

    def emit_passed(x, j, res):
        pas_s[x * YB + j] = res.astype(BF16)

    transport(halo_s, True, emit_passed)
    start_exchange(pas_s, pas_relay, pas_r, 1)

    def spread(g, _):
        rows = pl.ds(pl.multiple_of(g * LANES, LANES), LANES)
        ws[rows, :] = jnp.broadcast_to(shape_ref[pl.ds(g, 1), :], (LANES, LANES)).T
        wf[rows, :] = jnp.broadcast_to(flux_ref[pl.ds(g, 1), :], (LANES, LANES)).T
        return 0

    lax.fori_loop(0, 2048 // LANES, spread, 0)
    flags = flag_ref[...].astype(F32)
    gain = acc_ref[...] * flags

    def tile_rows(t):
        return pl.ds(pl.multiple_of(t * TILE, TILE), TILE)

    def tile_blocks(t):
        return pl.ds(pl.multiple_of(t * PER, PER), PER)

    def fold(a):
        return jnp.sum(a.reshape(TILE // 8, 8, LANES), axis=0)

    loads[2].wait()
    relay_exchange(cot_relay, cot_r, 0)
    wait_blocks(cot_r, recv_sem.at[0], NB - 8)
    cot_all = cot_r.reshape(2048, LANES)

    def adjoint_tile(t, total):
        rows = tile_rows(t)
        h = jnp.dot(cmat[rows, :], cot_all[...], preferred_element_type=F32)
        h = cot_all[rows, :].astype(F32) + h
        hbuf[rows, :] = h
        return total + fold(ws[rows, :] * h)

    total = lax.fori_loop(0, NT, adjoint_tile, jnp.zeros((8, LANES), F32))
    weighted = jnp.sum(total, axis=0, keepdims=True)

    def adjoint_out(k, _):
        rows = tile_rows(k)
        h = hbuf[rows, :]
        g = h + gain * (wf[rows, :] * weighted - h)
        adj_s[tile_blocks(k)] = g.astype(BF16).reshape(PER, VL, LANES)
        return 0

    lax.fori_loop(0, NT, adjoint_out, 0)
    send_all(adj_s, 0, halo_g, YB, 2)
    halo_g[YB + me] = adj_s[me]

    relay_exchange(pas_relay, pas_r, 1)
    wait_blocks(pas_r, recv_sem.at[1], NB - 8)
    pas_all = pas_r.reshape(2048, LANES)

    def density_tile(t, total):
        rows = tile_rows(t)
        return total + fold(wf[rows, :] * pas_all[rows, :].astype(F32))

    total = lax.fori_loop(0, NT, density_tile, jnp.zeros((8, LANES), F32))
    density = jnp.sum(total, axis=0, keepdims=True)

    def relax_block(g, total):
        rows = pl.ds(pl.multiple_of(g * LANES, LANES), LANES)
        moved = pas_all[rows, :].astype(F32)
        target = ws[rows, :] * density - moved
        relaxed = moved + gain * target
        xbuf[rows, :] = relaxed
        rt[:, rows] = relaxed.T.astype(BF16)
        return total + jnp.sum((hbuf[rows, :] * target).reshape(LANES // 8, 8, LANES), axis=0)

    total = lax.fori_loop(0, 2048 // LANES, relax_block, jnp.zeros((8, LANES), F32))
    sens_ref[...] = flags * jnp.sum(total, axis=0, keepdims=True)

    def forward_tile(k, _):
        t = column_of(k)
        rows = tile_rows(t)
        mixed = jnp.dot(rt[...], cmat[:, rows], preferred_element_type=F32)
        adv = xbuf[rows, :] + mixed.T
        adv_s[tile_blocks(t)] = adv.astype(BF16).reshape(PER, VL, LANES)

        @pl.when(k > 0)
        def _():
            send_column(adv_s, adv_r, 3, k - 1)

        return 0

    lax.fori_loop(0, NT, forward_tile, 0)
    send_column(adv_s, adv_r, 3, NT - 1)
    adv_r[me] = adv_s[me]

    wait_blocks(halo_g, recv_sem.at[2])
    face_g = face(halo_g, 1)
    face_g.start()
    face_g.wait()

    def emit_previous(x, j, res):
        turn[j, pl.ds(x, VL, stride=SLAB), :] = res

    transport(halo_g, False, emit_previous)
    out_rows(prev_ref)

    wait_blocks(adv_r, recv_sem.at[3])

    def unpack(x, _):
        for j in range(YB):
            turn[j, pl.ds(x, VL, stride=SLAB), :] = adv_r[x * YB + j].astype(F32)
        return 0

    lax.fori_loop(0, SLAB, unpack, 0, unroll=2)
    out_rows(adv_ref)

    for k, buf in enumerate((cot_s, pas_s)):
        wait_blocks(buf, line_ss.at[k], NB - PER)
        wait_blocks(buf, send_sem.at[k], NB - 8)
    for k, buf in ((2, adj_s), (3, adv_s)):
        wait_blocks(buf, send_sem.at[k])


def write_kernel(a_ref, b_ref, c_ref, a_out, b_out, c_out, sems):
    pairs = ((a_ref, a_out), (b_ref, b_out), (c_ref, c_out))
    copies = [pltpu.make_async_copy(src, dst, sems.at[i]) for i, (src, dst) in enumerate(pairs)]
    for c in copies:
        c.start()
    for c in copies:
        c.wait()


def body(state, cotangent, collision, wall_shape, flux_weight, courant, upwind_bits, accommodation, wall_flags):
    vm = pl.BlockSpec(memory_space=pltpu.VMEM)
    hb = pl.BlockSpec(memory_space=pltpu.HBM)
    blocks = pltpu.VMEM((NB, VL, LANES), BF16)
    full = pltpu.VMEM((2048, LANES), F32)
    results = pl.pallas_call(
        step_kernel,
        name="step",
        out_shape=(
            jax.ShapeDtypeStruct(state.shape, BF16),
            jax.ShapeDtypeStruct(state.shape, BF16),
            jax.ShapeDtypeStruct(accommodation.shape, F32),
        ),
        in_specs=[hb] * 9,
        out_specs=(vm, vm, vm),
        scratch_shapes=[
            pltpu.VMEM((16, LANES), F32),
            pltpu.VMEM((16, LANES), F32),
            pltpu.VMEM(courant.shape, F32),
            pltpu.VMEM(upwind_bits.shape, jnp.int32),
            pltpu.VMEM(accommodation.shape, F32),
            pltpu.VMEM(wall_flags.shape, jnp.int32),
            pltpu.VMEM(state.shape, BF16),
            pltpu.VMEM(state.shape, BF16),
            pltpu.VMEM(collision.shape, BF16),
            pltpu.VMEM((YB, VL * SLAB, LANES), F32),
            pltpu.VMEM((NB + 2 * YB, VL, LANES), BF16),
            pltpu.VMEM((NB + 2 * YB, VL, LANES), BF16),
            *[blocks] * 7,
            *[full] * 4,
            pltpu.VMEM((LANES, 2048), BF16),
            pltpu.VMEM((3, VL, LANES), F32),
            pltpu.VMEM((3, VL, LANES), F32),
            pltpu.SemaphoreType.DMA((9,)),
            pltpu.SemaphoreType.DMA((4,)),
            pltpu.SemaphoreType.DMA((4,)),
            pltpu.SemaphoreType.DMA((2,)),
            pltpu.SemaphoreType.DMA((2,)),
            pltpu.SemaphoreType.DMA((2,)),
            pltpu.SemaphoreType.DMA((2, 8)),
            pltpu.VMEM((8, 8, 2, VL, LANES), BF16),
            pltpu.VMEM((8, 8, 2, VL, LANES), BF16),
        ],
        compiler_params=pltpu.CompilerParams(
            collective_id=0, has_side_effects=True, vmem_limit_bytes=32 * 1024 * 1024
        ),
    )(
        *[
            pltpu.with_memory_space_constraint(a, pltpu.HBM)
            for a in (
                state, cotangent, collision, wall_shape.reshape(16, LANES), flux_weight.reshape(16, LANES),
                courant, upwind_bits, accommodation, wall_flags,
            )
        ]
    )
    return pl.pallas_call(
        write_kernel,
        name="write",
        out_shape=tuple(jax.ShapeDtypeStruct(r.shape, r.dtype) for r in results),
        in_specs=[vm] * 3,
        out_specs=(hb, hb, hb),
        scratch_shapes=[pltpu.SemaphoreType.DMA((3,))],
        compiler_params=pltpu.CompilerParams(vmem_limit_bytes=1024 * 1024),
    )(*results)


def solution(mesh):
    return jax.shard_map(
        body,
        mesh=mesh,
        in_specs=(
            P("vert", "sa", None),
            P("vert", "sa", None),
            P(),
            P(),
            P(),
            P(None, "vert"),
            P(None, "vert"),
            P(("vert", "sa"), None),
            P(("vert", "sa"), None),
        ),
        out_specs=(P("vert", "sa", None), P("vert", "sa", None), P(("vert", "sa"), None)),
        check_vma=False,
    )
```

```python
import jax
import jax.numpy as jnp
from jax import lax
from jax.experimental import pallas as pl
from jax.experimental.pallas import tpu as pltpu
from jax.sharding import PartitionSpec as P

MESH = pl.DeviceIdType.MESH
F32 = jnp.float32
BF16 = jnp.bfloat16
NZ = 32
LANES = 128
VL = 16
SLAB = 16
YB = 8
NB = SLAB * YB
TILE = 256
PER = TILE // VL
NT = 2048 // TILE
FAR_COLUMNS = ((1, 2), (1, 3), (1, 1), (1, 0), (0, 2), (0, 3), (0, 1), (0, 0))


def column(row, n):
    r = lax.broadcasted_iota(jnp.int32, (n, n), 0)
    c = lax.broadcasted_iota(jnp.int32, (n, n), 1)
    one = jnp.sum(jnp.where(r == c, jnp.broadcast_to(row, (n, n)), 0.0), axis=1, keepdims=True)
    return jnp.broadcast_to(one, (n, LANES))


def step_kernel(
    state_ref, cot_ref, coll_ref, shape_hbm, flux_hbm, cour_hbm, bits_hbm, acc_hbm, flag_hbm,
    adv_ref, prev_ref, sens_ref,
    shape_ref, flux_ref, cour_ref, bits_ref, acc_ref, flag_ref,
    svm, cvm, cmat, turn, halo_s, halo_g,
    cot_s, pas_s, adj_s, adv_s, cot_r, pas_r, adv_r,
    ws, wf, hbuf, xbuf, rt, coef, masks,
    load_sem, send_sem, recv_sem, face_ss, face_rs, line_sem, all_in, relay,
):
    me = lax.axis_index("vert")
    sa = lax.axis_index("sa")
    my_y, my_x, my_z, my_core = me // 64, (me // PER) % 4, (me // 2) % 8, me % 2
    my_column = [(my_y + dy) % 2 * 4 + (my_x + dx) % 4 for dy, dx in FAR_COLUMNS]
    my_cores = [(my_core + 1) % 2, my_core]
    near = [c * PER + core for c in my_column for core in my_cores]

    loads = [
        pltpu.make_async_copy(cot_ref, cvm, load_sem.at[0]),
        pltpu.make_async_copy(state_ref, svm, load_sem.at[1]),
        pltpu.make_async_copy(coll_ref, cmat, load_sem.at[2]),
    ]
    small = (
        (shape_hbm, shape_ref), (flux_hbm, flux_ref), (cour_hbm, cour_ref),
        (bits_hbm, bits_ref), (acc_hbm, acc_ref), (flag_hbm, flag_ref),
    )
    loads += [pltpu.make_async_copy(src, dst, load_sem.at[3 + i]) for i, (src, dst) in enumerate(small)]
    for c in loads:
        c.start()

    barrier = pltpu.get_barrier_semaphore()

    def far_z(i):
        return (my_z + 4 + i // 2 - (i % 2) * i) % 8

    def each_peer(visit, first=0):
        def place(i, _):
            z2 = far_z(i) * 2
            for n in near[:-1]:
                visit(z2 + n)

            @pl.when(i < 7)
            def _():
                visit(z2 + near[-1])

            return 0

        lax.fori_loop(first, 8, place, 0)

    def greet(d):
        pl.semaphore_signal(barrier, inc=1, device_id={"vert": d}, device_id_type=MESH)

    my_col = my_y * 4 + my_x
    for i in range(7):
        greet(my_col * PER + far_z(i) * 2 + my_core)
    for n in near[:-1]:
        greet(n + my_z * 2)
    pl.semaphore_signal(barrier, inc=1, device_id={"sa": 1 - sa}, device_id_type=MESH)
    for c in loads[3:]:
        c.wait()

    for d in range(3):
        coef[d] = column(cour_ref[d : d + 1, :], VL)
        masks[d] = column(bits_ref[d : d + 1, :].astype(F32), VL)
    zero_plane = jnp.zeros((YB, VL, LANES), BF16)
    lone = sa * (NB + YB)
    halo_s[pl.ds(lone, YB)] = zero_plane
    halo_g[pl.ds(lone, YB)] = zero_plane

    def to_blocks(src, dst, base):
        def rows_in(v, _):
            plane = src[v].astype(F32)
            for j in range(YB):
                turn[j, pl.ds(v, SLAB, stride=VL), :] = plane[:, j * LANES : (j + 1) * LANES]
            return 0

        lax.fori_loop(0, VL, rows_in, 0, unroll=4)

        def planes_out(x, _):
            for j in range(YB):
                part = turn[j, pl.ds(pl.multiple_of(x * VL, VL), VL), :]
                dst[base + x * YB + j] = part.astype(BF16)
            return 0

        lax.fori_loop(0, SLAB, planes_out, 0, unroll=2)

    def send(src, src_base, dst, dst_base, phase, d):
        pltpu.make_async_remote_copy(
            src_ref=src.at[src_base + d],
            dst_ref=dst.at[dst_base + me],
            send_sem=send_sem.at[phase],
            recv_sem=recv_sem.at[phase],
            device_id={"vert": d},
            device_id_type=MESH,
        ).start()

    def column_of(k):
        dx = 2 + k % 4 - (k % 4 // 2) * (2 * (k % 4) - 1)
        return (my_y + 1 - k // 4) % 2 * 4 + (my_x + dx) % 4

    def send_column(src, dst, phase, k):
        first = column_of(k) * PER

        def place(i, _):
            z2 = far_z(i) * 2 + first
            send(src, 0, dst, 0, phase, z2 + my_cores[0])

            @pl.when(i + k < 14)
            def _():
                send(src, 0, dst, 0, phase, z2 + my_cores[1])

            return 0

        lax.fori_loop(0, 8, place, 0)

    def send_all(src, src_base, dst, dst_base, phase, first=0):
        each_peer(lambda d: send(src, src_base, dst, dst_base, phase, d), first)

    def wait_blocks(ref, sem, blocks=NB - 1):
        part = ref.at[pl.ds(0, blocks)]
        pltpu.make_async_copy(part, part, sem).wait()

    def face(buf, k):
        return pltpu.make_async_remote_copy(
            src_ref=buf.at[pl.ds(YB + (NB - YB) * (1 - sa), YB)],
            dst_ref=buf.at[pl.ds((NB + YB) * sa, YB)],
            send_sem=face_ss.at[k],
            recv_sem=face_rs.at[k],
            device_id={"sa": 1 - sa},
            device_id_type=MESH,
        )

    lane = lax.broadcasted_iota(jnp.int32, (VL, LANES), 1)
    z_at = lane % NZ

    def transport(buf, forward, emit):
        def plane(x, _):
            base = x * YB
            mid = [buf[base + YB + j].astype(F32) for j in range(YB)]
            up32 = [pltpu.roll(m, NZ, 1) for m in mid]
            dn32 = [pltpu.roll(m, LANES - NZ, 1) for m in mid]
            zero = jnp.zeros((VL, LANES), F32)
            for j in range(YB):
                m = mid[j]
                minus = (
                    buf[base + j].astype(F32),
                    jnp.where(lane < NZ, up32[j - 1] if j else zero, up32[j]),
                    jnp.where(z_at != 0, pltpu.roll(m, 1, 1), 0.0),
                )
                plus = (
                    buf[base + 2 * YB + j].astype(F32),
                    jnp.where(lane >= LANES - NZ, dn32[j + 1] if j < YB - 1 else zero, dn32[j]),
                    jnp.where(z_at != NZ - 1, pltpu.roll(m, LANES - 1, 1), 0.0),
                )
                res = m
                for d in range(3):
                    up = masks[d] == 1.0
                    donor = jnp.where(up, minus[d], plus[d]) if forward else jnp.where(up, plus[d], minus[d])
                    res = res - coef[d] * (m - donor)
                emit(x, j, res)
            return 0

        lax.fori_loop(0, SLAB, plane, 0)

    def out_rows(dst):
        def one(v, _):
            for j in range(YB):
                rows = turn[j, pl.ds(pl.multiple_of(v * SLAB, SLAB), SLAB), :]
                dst[v, :, j * LANES : (j + 1) * LANES] = rows.astype(BF16)
            return 0

        lax.fori_loop(0, VL, one, 0, unroll=2)

    loads[0].wait()
    to_blocks(cvm, cot_s, 0)

    pl.semaphore_wait(barrier, 23)
    for n in near[:-1]:
        pl.semaphore_signal(all_in, inc=1, device_id={"vert": n + my_z * 2}, device_id_type=MESH)
    z_far = (my_z + 4) % 8
    line = pltpu.make_async_remote_copy(
        src_ref=cot_s.reshape(8, 8, 2, VL, LANES).at[:, z_far],
        dst_ref=relay,
        send_sem=line_sem.at[0],
        recv_sem=line_sem.at[1],
        device_id={"vert": my_col * PER + z_far * 2 + my_core},
        device_id_type=MESH,
    )
    line.start()
    loads[1].wait()
    to_blocks(svm, halo_s, YB)
    face_s = face(halo_s, 0)
    face_s.start()

    pl.semaphore_wait(all_in, 15)
    send_all(cot_s, 0, cot_r, 0, 0, first=1)
    cot_r[me] = cot_s[me]

    face_s.wait()

    def emit_passed(x, j, res):
        pas_s[x * YB + j] = res.astype(BF16)

    transport(halo_s, True, emit_passed)
    line.wait()
    came_from = my_col * PER + z_far * 2 + my_core
    for col in my_column:
        for core in my_cores:
            if col is my_column[-1] and core is my_cores[-1]:
                continue
            pltpu.make_async_remote_copy(
                src_ref=relay.at[col, core],
                dst_ref=cot_r.at[came_from],
                send_sem=send_sem.at[0],
                recv_sem=recv_sem.at[0],
                device_id={"vert": col * PER + my_z * 2 + core},
                device_id_type=MESH,
            ).start()
    cot_r[came_from] = relay[my_col, my_core]
    send_all(pas_s, 0, pas_r, 0, 1)
    pas_r[me] = pas_s[me]

    def spread(g, _):
        rows = pl.ds(pl.multiple_of(g * LANES, LANES), LANES)
        ws[rows, :] = jnp.broadcast_to(shape_ref[pl.ds(g, 1), :], (LANES, LANES)).T
        wf[rows, :] = jnp.broadcast_to(flux_ref[pl.ds(g, 1), :], (LANES, LANES)).T
        return 0

    lax.fori_loop(0, 2048 // LANES, spread, 0)
    flags = flag_ref[...].astype(F32)
    gain = acc_ref[...] * flags

    def tile_rows(t):
        return pl.ds(pl.multiple_of(t * TILE, TILE), TILE)

    def tile_blocks(t):
        return pl.ds(pl.multiple_of(t * PER, PER), PER)

    def fold(a):
        return jnp.sum(a.reshape(TILE // 8, 8, LANES), axis=0)

    loads[2].wait()
    wait_blocks(cot_r, recv_sem.at[0], NB - 2)
    cot_all = cot_r.reshape(2048, LANES)

    def adjoint_tile(t, total):
        rows = tile_rows(t)
        h = jnp.dot(cmat[rows, :], cot_all[...], preferred_element_type=F32)
        h = cot_all[rows, :].astype(F32) + h
        hbuf[rows, :] = h
        return total + fold(ws[rows, :] * h)

    total = lax.fori_loop(0, NT, adjoint_tile, jnp.zeros((8, LANES), F32))
    weighted = jnp.sum(total, axis=0, keepdims=True)

    def adjoint_out(k, _):
        rows = tile_rows(k)
        h = hbuf[rows, :]
        g = h + gain * (wf[rows, :] * weighted - h)
        adj_s[tile_blocks(k)] = g.astype(BF16).reshape(PER, VL, LANES)
        return 0

    lax.fori_loop(0, NT, adjoint_out, 0)
    send_all(adj_s, 0, halo_g, YB, 2)
    halo_g[YB + me] = adj_s[me]

    wait_blocks(pas_r, recv_sem.at[1])
    pas_all = pas_r.reshape(2048, LANES)

    def density_tile(t, total):
        rows = tile_rows(t)
        return total + fold(wf[rows, :] * pas_all[rows, :].astype(F32))

    total = lax.fori_loop(0, NT, density_tile, jnp.zeros((8, LANES), F32))
    density = jnp.sum(total, axis=0, keepdims=True)

    def relax_block(g, total):
        rows = pl.ds(pl.multiple_of(g * LANES, LANES), LANES)
        moved = pas_all[rows, :].astype(F32)
        target = ws[rows, :] * density - moved
        relaxed = moved + gain * target
        xbuf[rows, :] = relaxed
        rt[:, rows] = relaxed.T.astype(BF16)
        return total + jnp.sum((hbuf[rows, :] * target).reshape(LANES // 8, 8, LANES), axis=0)

    total = lax.fori_loop(0, 2048 // LANES, relax_block, jnp.zeros((8, LANES), F32))
    sens_ref[...] = flags * jnp.sum(total, axis=0, keepdims=True)

    def forward_tile(k, _):
        t = column_of(k)
        rows = tile_rows(t)
        mixed = jnp.dot(rt[...], cmat[:, rows], preferred_element_type=F32)
        adv = xbuf[rows, :] + mixed.T
        adv_s[tile_blocks(t)] = adv.astype(BF16).reshape(PER, VL, LANES)

        @pl.when(k > 0)
        def _():
            send_column(adv_s, adv_r, 3, k - 1)

        return 0

    lax.fori_loop(0, NT, forward_tile, 0)
    send_column(adv_s, adv_r, 3, NT - 1)
    adv_r[me] = adv_s[me]

    wait_blocks(halo_g, recv_sem.at[2])
    face_g = face(halo_g, 1)
    face_g.start()
    face_g.wait()

    def emit_previous(x, j, res):
        turn[j, pl.ds(x, VL, stride=SLAB), :] = res

    transport(halo_g, False, emit_previous)
    out_rows(prev_ref)

    wait_blocks(adv_r, recv_sem.at[3])

    def unpack(x, _):
        for j in range(YB):
            turn[j, pl.ds(x, VL, stride=SLAB), :] = adv_r[x * YB + j].astype(F32)
        return 0

    lax.fori_loop(0, SLAB, unpack, 0, unroll=2)
    out_rows(adv_ref)

    for phase, buf in enumerate((cot_s, pas_s, adj_s, adv_s)):
        wait_blocks(buf, send_sem.at[phase], NB - 1 - (phase == 0))


def write_kernel(a_ref, b_ref, c_ref, a_out, b_out, c_out, sems):
    pairs = ((a_ref, a_out), (b_ref, b_out), (c_ref, c_out))
    copies = [pltpu.make_async_copy(src, dst, sems.at[i]) for i, (src, dst) in enumerate(pairs)]
    for c in copies:
        c.start()
    for c in copies:
        c.wait()


def body(state, cotangent, collision, wall_shape, flux_weight, courant, upwind_bits, accommodation, wall_flags):
    vm = pl.BlockSpec(memory_space=pltpu.VMEM)
    hb = pl.BlockSpec(memory_space=pltpu.HBM)
    blocks = pltpu.VMEM((NB, VL, LANES), BF16)
    full = pltpu.VMEM((2048, LANES), F32)
    results = pl.pallas_call(
        step_kernel,
        name="step",
        out_shape=(
            jax.ShapeDtypeStruct(state.shape, BF16),
            jax.ShapeDtypeStruct(state.shape, BF16),
            jax.ShapeDtypeStruct(accommodation.shape, F32),
        ),
        in_specs=[hb] * 9,
        out_specs=(vm, vm, vm),
        scratch_shapes=[
            pltpu.VMEM((16, LANES), F32),
            pltpu.VMEM((16, LANES), F32),
            pltpu.VMEM(courant.shape, F32),
            pltpu.VMEM(upwind_bits.shape, jnp.int32),
            pltpu.VMEM(accommodation.shape, F32),
            pltpu.VMEM(wall_flags.shape, jnp.int32),
            pltpu.VMEM(state.shape, BF16),
            pltpu.VMEM(state.shape, BF16),
            pltpu.VMEM(collision.shape, BF16),
            pltpu.VMEM((YB, VL * SLAB, LANES), F32),
            pltpu.VMEM((NB + 2 * YB, VL, LANES), BF16),
            pltpu.VMEM((NB + 2 * YB, VL, LANES), BF16),
            *[blocks] * 7,
            *[full] * 4,
            pltpu.VMEM((LANES, 2048), BF16),
            pltpu.VMEM((3, VL, LANES), F32),
            pltpu.VMEM((3, VL, LANES), F32),
            pltpu.SemaphoreType.DMA((9,)),
            pltpu.SemaphoreType.DMA((4,)),
            pltpu.SemaphoreType.DMA((4,)),
            pltpu.SemaphoreType.DMA((2,)),
            pltpu.SemaphoreType.DMA((2,)),
            pltpu.SemaphoreType.DMA((2,)),
            pltpu.SemaphoreType.REGULAR,
            pltpu.VMEM((8, 2, VL, LANES), BF16),
        ],
        compiler_params=pltpu.CompilerParams(
            collective_id=0, has_side_effects=True, vmem_limit_bytes=32 * 1024 * 1024
        ),
    )(
        *[
            pltpu.with_memory_space_constraint(a, pltpu.HBM)
            for a in (
                state, cotangent, collision, wall_shape.reshape(16, LANES), flux_weight.reshape(16, LANES),
                courant, upwind_bits, accommodation, wall_flags,
            )
        ]
    )
    return pl.pallas_call(
        write_kernel,
        name="write",
        out_shape=tuple(jax.ShapeDtypeStruct(r.shape, r.dtype) for r in results),
        in_specs=[vm] * 3,
        out_specs=(hb, hb, hb),
        scratch_shapes=[pltpu.SemaphoreType.DMA((3,))],
        compiler_params=pltpu.CompilerParams(vmem_limit_bytes=1024 * 1024),
    )(*results)


def solution(mesh):
    return jax.shard_map(
        body,
        mesh=mesh,
        in_specs=(
            P("vert", "sa", None),
            P("vert", "sa", None),
            P(),
            P(),
            P(),
            P(None, "vert"),
            P(None, "vert"),
            P(("vert", "sa"), None),
            P(("vert", "sa"), None),
        ),
        out_specs=(P("vert", "sa", None), P("vert", "sa", None), P(("vert", "sa"), None)),
        check_vma=False,
    )
```

```python
import jax
import jax.numpy as jnp
from jax import lax
from jax.experimental import pallas as pl
from jax.experimental.pallas import tpu as pltpu
from jax.sharding import PartitionSpec as P

MESH = pl.DeviceIdType.MESH
F32 = jnp.float32
BF16 = jnp.bfloat16
NZ = 32
LANES = 128
VL = 16
SLAB = 16
YB = 8
NB = SLAB * YB
TILE = 256
PER = TILE // VL
NT = 2048 // TILE
FAR_COLUMNS = ((1, 2), (1, 3), (1, 1), (1, 0), (0, 2), (0, 3), (0, 1), (0, 0))


def column(row, n):
    r = lax.broadcasted_iota(jnp.int32, (n, n), 0)
    c = lax.broadcasted_iota(jnp.int32, (n, n), 1)
    one = jnp.sum(jnp.where(r == c, jnp.broadcast_to(row, (n, n)), 0.0), axis=1, keepdims=True)
    return jnp.broadcast_to(one, (n, LANES))


def step_kernel(
    state_ref, cot_ref, coll_ref, shape_hbm, flux_hbm, cour_hbm, bits_hbm, acc_hbm, flag_hbm,
    adv_ref, prev_ref, sens_ref,
    shape_ref, flux_ref, cour_ref, bits_ref, acc_ref, flag_ref,
    svm, cvm, cmat, turn, halo_s, halo_g,
    cot_s, pas_s, adj_s, adv_s, cot_r, pas_r, adv_r,
    ws, wf, hbuf, xbuf, rt, coef, masks,
    load_sem, send_sem, recv_sem, face_ss, face_rs, line_sem, all_in, relay,
):
    me = lax.axis_index("vert")
    sa = lax.axis_index("sa")
    my_y, my_x, my_z, my_core = me // 64, (me // PER) % 4, (me // 2) % 8, me % 2
    my_column = [(my_y + dy) % 2 * 4 + (my_x + dx) % 4 for dy, dx in FAR_COLUMNS]
    my_cores = [(my_core + 1) % 2, my_core]
    near = [c * PER + core for c in my_column for core in my_cores]

    loads = [
        pltpu.make_async_copy(cot_ref, cvm, load_sem.at[0]),
        pltpu.make_async_copy(state_ref, svm, load_sem.at[1]),
        pltpu.make_async_copy(coll_ref, cmat, load_sem.at[2]),
    ]
    small = (
        (shape_hbm, shape_ref), (flux_hbm, flux_ref), (cour_hbm, cour_ref),
        (bits_hbm, bits_ref), (acc_hbm, acc_ref), (flag_hbm, flag_ref),
    )
    loads += [pltpu.make_async_copy(src, dst, load_sem.at[3 + i]) for i, (src, dst) in enumerate(small)]
    for c in loads:
        c.start()

    barrier = pltpu.get_barrier_semaphore()

    def far_z(i):
        return (my_z + 4 + i // 2 - (i % 2) * i) % 8

    def each_peer(visit, first=0):
        count = 8 - first

        def turn_of(i, _):
            for j, n in enumerate(near[:-1]):
                visit(far_z(first + (i + j) % count) * 2 + n)

            @pl.when((i + 15) % count < count - 1)
            def _():
                visit(far_z(first + (i + 15) % count) * 2 + near[-1])

            return 0

        lax.fori_loop(0, count, turn_of, 0)

    def greet(d):
        pl.semaphore_signal(barrier, inc=1, device_id={"vert": d}, device_id_type=MESH)

    my_col = my_y * 4 + my_x
    for i in range(7):
        greet(my_col * PER + far_z(i) * 2 + my_core)
    for n in near[:-1]:
        greet(n + my_z * 2)
    pl.semaphore_signal(barrier, inc=1, device_id={"sa": 1 - sa}, device_id_type=MESH)
    for c in loads[3:]:
        c.wait()

    for d in range(3):
        coef[d] = column(cour_ref[d : d + 1, :], VL)
        masks[d] = column(bits_ref[d : d + 1, :].astype(F32), VL)
    zero_plane = jnp.zeros((YB, VL, LANES), BF16)
    lone = sa * (NB + YB)
    halo_s[pl.ds(lone, YB)] = zero_plane
    halo_g[pl.ds(lone, YB)] = zero_plane

    def to_blocks(src, dst, base):
        def rows_in(v, _):
            plane = src[v].astype(F32)
            for j in range(YB):
                turn[j, pl.ds(v, SLAB, stride=VL), :] = plane[:, j * LANES : (j + 1) * LANES]
            return 0

        lax.fori_loop(0, VL, rows_in, 0, unroll=4)

        def planes_out(x, _):
            for j in range(YB):
                part = turn[j, pl.ds(pl.multiple_of(x * VL, VL), VL), :]
                dst[base + x * YB + j] = part.astype(BF16)
            return 0

        lax.fori_loop(0, SLAB, planes_out, 0, unroll=2)

    def send(src, src_base, dst, dst_base, phase, d):
        pltpu.make_async_remote_copy(
            src_ref=src.at[src_base + d],
            dst_ref=dst.at[dst_base + me],
            send_sem=send_sem.at[phase],
            recv_sem=recv_sem.at[phase],
            device_id={"vert": d},
            device_id_type=MESH,
        ).start()

    def column_of(k):
        dx = 2 + k % 4 - (k % 4 // 2) * (2 * (k % 4) - 1)
        return (my_y + 1 - k // 4) % 2 * 4 + (my_x + dx) % 4

    def send_column(src, dst, phase, k):
        first = column_of(k) * PER

        def place(i, _):
            z2 = far_z(i) * 2 + first
            send(src, 0, dst, 0, phase, z2 + my_cores[0])

            @pl.when(i + k < 14)
            def _():
                send(src, 0, dst, 0, phase, z2 + my_cores[1])

            return 0

        lax.fori_loop(0, 8, place, 0)

    def send_all(src, src_base, dst, dst_base, phase, first=0):
        each_peer(lambda d: send(src, src_base, dst, dst_base, phase, d), first)

    def wait_blocks(ref, sem, blocks=NB - 1):
        part = ref.at[pl.ds(0, blocks)]
        pltpu.make_async_copy(part, part, sem).wait()

    def face(buf, k):
        return pltpu.make_async_remote_copy(
            src_ref=buf.at[pl.ds(YB + (NB - YB) * (1 - sa), YB)],
            dst_ref=buf.at[pl.ds((NB + YB) * sa, YB)],
            send_sem=face_ss.at[k],
            recv_sem=face_rs.at[k],
            device_id={"sa": 1 - sa},
            device_id_type=MESH,
        )

    lane = lax.broadcasted_iota(jnp.int32, (VL, LANES), 1)
    z_at = lane % NZ

    def transport(buf, forward, emit):
        def plane(x, _):
            base = x * YB
            mid = [buf[base + YB + j].astype(F32) for j in range(YB)]
            up32 = [pltpu.roll(m, NZ, 1) for m in mid]
            dn32 = [pltpu.roll(m, LANES - NZ, 1) for m in mid]
            zero = jnp.zeros((VL, LANES), F32)
            for j in range(YB):
                m = mid[j]
                minus = (
                    buf[base + j].astype(F32),
                    jnp.where(lane < NZ, up32[j - 1] if j else zero, up32[j]),
                    jnp.where(z_at != 0, pltpu.roll(m, 1, 1), 0.0),
                )
                plus = (
                    buf[base + 2 * YB + j].astype(F32),
                    jnp.where(lane >= LANES - NZ, dn32[j + 1] if j < YB - 1 else zero, dn32[j]),
                    jnp.where(z_at != NZ - 1, pltpu.roll(m, LANES - 1, 1), 0.0),
                )
                res = m
                for d in range(3):
                    up = masks[d] == 1.0
                    donor = jnp.where(up, minus[d], plus[d]) if forward else jnp.where(up, plus[d], minus[d])
                    res = res - coef[d] * (m - donor)
                emit(x, j, res)
            return 0

        lax.fori_loop(0, SLAB, plane, 0)

    def out_rows(dst):
        def one(v, _):
            for j in range(YB):
                rows = turn[j, pl.ds(pl.multiple_of(v * SLAB, SLAB), SLAB), :]
                dst[v, :, j * LANES : (j + 1) * LANES] = rows.astype(BF16)
            return 0

        lax.fori_loop(0, VL, one, 0, unroll=2)

    loads[0].wait()
    to_blocks(cvm, cot_s, 0)

    pl.semaphore_wait(barrier, 23)
    for n in near[:-1]:
        pl.semaphore_signal(all_in, inc=1, device_id={"vert": n + my_z * 2}, device_id_type=MESH)
    z_far = (my_z + 4) % 8
    line = pltpu.make_async_remote_copy(
        src_ref=cot_s.reshape(8, 8, 2, VL, LANES).at[:, z_far],
        dst_ref=relay,
        send_sem=line_sem.at[0],
        recv_sem=line_sem.at[1],
        device_id={"vert": my_col * PER + z_far * 2 + my_core},
        device_id_type=MESH,
    )
    line.start()
    loads[1].wait()
    to_blocks(svm, halo_s, YB)
    face_s = face(halo_s, 0)
    face_s.start()

    pl.semaphore_wait(all_in, 15)
    send_all(cot_s, 0, cot_r, 0, 0, first=1)
    cot_r[me] = cot_s[me]

    face_s.wait()

    def emit_passed(x, j, res):
        pas_s[x * YB + j] = res.astype(BF16)

    transport(halo_s, True, emit_passed)
    line.wait()
    came_from = my_col * PER + z_far * 2 + my_core
    for col in my_column:
        for core in my_cores:
            if col is my_column[-1] and core is my_cores[-1]:
                continue
            pltpu.make_async_remote_copy(
                src_ref=relay.at[col, core],
                dst_ref=cot_r.at[came_from],
                send_sem=send_sem.at[0],
                recv_sem=recv_sem.at[0],
                device_id={"vert": col * PER + my_z * 2 + core},
                device_id_type=MESH,
            ).start()
    cot_r[came_from] = relay[my_col, my_core]
    send_all(pas_s, 0, pas_r, 0, 1)
    pas_r[me] = pas_s[me]

    def spread(g, _):
        rows = pl.ds(pl.multiple_of(g * LANES, LANES), LANES)
        ws[rows, :] = jnp.broadcast_to(shape_ref[pl.ds(g, 1), :], (LANES, LANES)).T
        wf[rows, :] = jnp.broadcast_to(flux_ref[pl.ds(g, 1), :], (LANES, LANES)).T
        return 0

    lax.fori_loop(0, 2048 // LANES, spread, 0)
    flags = flag_ref[...].astype(F32)
    gain = acc_ref[...] * flags

    def tile_rows(t):
        return pl.ds(pl.multiple_of(t * TILE, TILE), TILE)

    def tile_blocks(t):
        return pl.ds(pl.multiple_of(t * PER, PER), PER)

    def fold(a):
        return jnp.sum(a.reshape(TILE // 8, 8, LANES), axis=0)

    loads[2].wait()
    wait_blocks(cot_r, recv_sem.at[0], NB - 2)
    cot_all = cot_r.reshape(2048, LANES)

    def adjoint_tile(t, total):
        rows = tile_rows(t)
        h = jnp.dot(cmat[rows, :], cot_all[...], preferred_element_type=F32)
        h = cot_all[rows, :].astype(F32) + h
        hbuf[rows, :] = h
        return total + fold(ws[rows, :] * h)

    total = lax.fori_loop(0, NT, adjoint_tile, jnp.zeros((8, LANES), F32))
    weighted = jnp.sum(total, axis=0, keepdims=True)

    def adjoint_out(k, _):
        rows = tile_rows(k)
        h = hbuf[rows, :]
        g = h + gain * (wf[rows, :] * weighted - h)
        adj_s[tile_blocks(k)] = g.astype(BF16).reshape(PER, VL, LANES)
        return 0

    lax.fori_loop(0, NT, adjoint_out, 0)
    send_all(adj_s, 0, halo_g, YB, 2)
    halo_g[YB + me] = adj_s[me]

    wait_blocks(pas_r, recv_sem.at[1])
    pas_all = pas_r.reshape(2048, LANES)

    def density_tile(t, total):
        rows = tile_rows(t)
        return total + fold(wf[rows, :] * pas_all[rows, :].astype(F32))

    total = lax.fori_loop(0, NT, density_tile, jnp.zeros((8, LANES), F32))
    density = jnp.sum(total, axis=0, keepdims=True)

    def relax_block(g, total):
        rows = pl.ds(pl.multiple_of(g * LANES, LANES), LANES)
        moved = pas_all[rows, :].astype(F32)
        target = ws[rows, :] * density - moved
        relaxed = moved + gain * target
        xbuf[rows, :] = relaxed
        rt[:, rows] = relaxed.T.astype(BF16)
        return total + jnp.sum((hbuf[rows, :] * target).reshape(LANES // 8, 8, LANES), axis=0)

    total = lax.fori_loop(0, 2048 // LANES, relax_block, jnp.zeros((8, LANES), F32))
    sens_ref[...] = flags * jnp.sum(total, axis=0, keepdims=True)

    def forward_tile(k, _):
        t = column_of(k)
        rows = tile_rows(t)
        mixed = jnp.dot(rt[...], cmat[:, rows], preferred_element_type=F32)
        adv = xbuf[rows, :] + mixed.T
        adv_s[tile_blocks(t)] = adv.astype(BF16).reshape(PER, VL, LANES)

        @pl.when(k > 0)
        def _():
            send_column(adv_s, adv_r, 3, k - 1)

        return 0

    lax.fori_loop(0, NT, forward_tile, 0)
    send_column(adv_s, adv_r, 3, NT - 1)
    adv_r[me] = adv_s[me]

    wait_blocks(halo_g, recv_sem.at[2])
    face_g = face(halo_g, 1)
    face_g.start()
    face_g.wait()

    def emit_previous(x, j, res):
        turn[j, pl.ds(x, VL, stride=SLAB), :] = res

    transport(halo_g, False, emit_previous)
    out_rows(prev_ref)

    wait_blocks(adv_r, recv_sem.at[3])

    def unpack(x, _):
        for j in range(YB):
            turn[j, pl.ds(x, VL, stride=SLAB), :] = adv_r[x * YB + j].astype(F32)
        return 0

    lax.fori_loop(0, SLAB, unpack, 0, unroll=2)
    out_rows(adv_ref)

    for phase, buf in enumerate((cot_s, pas_s, adj_s, adv_s)):
        wait_blocks(buf, send_sem.at[phase], NB - 1 - (phase == 0))


def write_kernel(a_ref, b_ref, c_ref, a_out, b_out, c_out, sems):
    pairs = ((a_ref, a_out), (b_ref, b_out), (c_ref, c_out))
    copies = [pltpu.make_async_copy(src, dst, sems.at[i]) for i, (src, dst) in enumerate(pairs)]
    for c in copies:
        c.start()
    for c in copies:
        c.wait()


def body(state, cotangent, collision, wall_shape, flux_weight, courant, upwind_bits, accommodation, wall_flags):
    vm = pl.BlockSpec(memory_space=pltpu.VMEM)
    hb = pl.BlockSpec(memory_space=pltpu.HBM)
    blocks = pltpu.VMEM((NB, VL, LANES), BF16)
    full = pltpu.VMEM((2048, LANES), F32)
    results = pl.pallas_call(
        step_kernel,
        name="step",
        out_shape=(
            jax.ShapeDtypeStruct(state.shape, BF16),
            jax.ShapeDtypeStruct(state.shape, BF16),
            jax.ShapeDtypeStruct(accommodation.shape, F32),
        ),
        in_specs=[hb] * 9,
        out_specs=(vm, vm, vm),
        scratch_shapes=[
            pltpu.VMEM((16, LANES), F32),
            pltpu.VMEM((16, LANES), F32),
            pltpu.VMEM(courant.shape, F32),
            pltpu.VMEM(upwind_bits.shape, jnp.int32),
            pltpu.VMEM(accommodation.shape, F32),
            pltpu.VMEM(wall_flags.shape, jnp.int32),
            pltpu.VMEM(state.shape, BF16),
            pltpu.VMEM(state.shape, BF16),
            pltpu.VMEM(collision.shape, BF16),
            pltpu.VMEM((YB, VL * SLAB, LANES), F32),
            pltpu.VMEM((NB + 2 * YB, VL, LANES), BF16),
            pltpu.VMEM((NB + 2 * YB, VL, LANES), BF16),
            *[blocks] * 7,
            *[full] * 4,
            pltpu.VMEM((LANES, 2048), BF16),
            pltpu.VMEM((3, VL, LANES), F32),
            pltpu.VMEM((3, VL, LANES), F32),
            pltpu.SemaphoreType.DMA((9,)),
            pltpu.SemaphoreType.DMA((4,)),
            pltpu.SemaphoreType.DMA((4,)),
            pltpu.SemaphoreType.DMA((2,)),
            pltpu.SemaphoreType.DMA((2,)),
            pltpu.SemaphoreType.DMA((2,)),
            pltpu.SemaphoreType.REGULAR,
            pltpu.VMEM((8, 2, VL, LANES), BF16),
        ],
        compiler_params=pltpu.CompilerParams(
            collective_id=0, has_side_effects=True, vmem_limit_bytes=32 * 1024 * 1024
        ),
    )(
        *[
            pltpu.with_memory_space_constraint(a, pltpu.HBM)
            for a in (
                state, cotangent, collision, wall_shape.reshape(16, LANES), flux_weight.reshape(16, LANES),
                courant, upwind_bits, accommodation, wall_flags,
            )
        ]
    )
    return pl.pallas_call(
        write_kernel,
        name="write",
        out_shape=tuple(jax.ShapeDtypeStruct(r.shape, r.dtype) for r in results),
        in_specs=[vm] * 3,
        out_specs=(hb, hb, hb),
        scratch_shapes=[pltpu.SemaphoreType.DMA((3,))],
        compiler_params=pltpu.CompilerParams(vmem_limit_bytes=1024 * 1024),
    )(*results)


def solution(mesh):
    return jax.shard_map(
        body,
        mesh=mesh,
        in_specs=(
            P("vert", "sa", None),
            P("vert", "sa", None),
            P(),
            P(),
            P(),
            P(None, "vert"),
            P(None, "vert"),
            P(("vert", "sa"), None),
            P(("vert", "sa"), None),
        ),
        out_specs=(P("vert", "sa", None), P("vert", "sa", None), P(("vert", "sa"), None)),
        check_vma=False,
    )
```
